32 devices in a mesh: dp: 16 (over z, y, core), tensor: 2 (over x).
Axes of the slice: x: 2, y: 2, z: 4, core: 2. Of those that a mesh axis runs over, the one named last changes fastest.
Arguments:
- tokens: bfloat16 [4096, 6144], P('dp', 'tensor'), may hold values from -6 to 6
- grad_out: bfloat16 [4096, 6144], P('dp', 'tensor'), may hold values from -6 to 6
- input_norm_gain: float32 [6144], replicated, may hold values from 0.1 to 1.9
- q_gain: float32 [128], replicated, may hold values from 0.1 to 1.9
- k_gain: float32 [128], replicated, may hold values from 0.1 to 1.9
- w_qkv: bfloat16 [3, 6144, 3072], P(None, 'dp', 'tensor'), may hold values from -0.078125 to 0.078125
- w_out: bfloat16 [3072, 6144], P('tensor', 'dp'), may hold values from -0.109375 to 0.109375
- pattern: int32 [24, 4, 2], P('tensor'), may hold values from 0 to 3, all different within a row
Outputs:
- tokens_grad: bfloat16 [4096, 6144], P('dp', 'tensor')
The draws below stay inside these ranges and needn't reach their ends.
All inputs are finite; a program needn't handle non-finite values.
Results may differ from the reference program's by a relative error of at most 0.015.
Values may be sent and summed in bfloat16 or wider, within the bound.
A program may use at most 192 MiB of HBM per device.

```python
import math
import jax
import jax.numpy as jnp
from jax import lax

D = 6144
HEADS = 24
HD = 128
SEQ = 256
BLK = 64
KSEL = 2
NQB = 4
TOKENS = 4096


def level_of(own_key, extent, cuts, least, high):
    factor_of = 1.0
    for position, parts in cuts:
        heights = jax.random.uniform(jax.random.fold_in(jax.random.fold_in(own_key, 6), position), (parts,), jnp.float32, least / len(cuts), high / len(cuts))
        factor_of = factor_of * jnp.repeat(jnp.exp(heights), extent[position] // parts).reshape((-1,) + (1,) * (len(extent) - 1 - position))
    return factor_of


def distinct(own_key, rows, number_of, top, lift):
    ranking = jax.random.permutation(jax.random.fold_in(own_key, 1), number_of)
    boost = ranking
    for power in range(3):
        boost = boost * boost // number_of
    boost = boost * lift // number_of
    tickets = jax.random.randint(jax.random.fold_in(own_key, 2), (rows, number_of), 0, 4096) + boost
    fixed_rows = jax.random.permutation(jax.random.fold_in(own_key, 3), rows)[jnp.arange(number_of) % rows]
    tickets = jnp.where(jnp.arange(rows)[:, None] == fixed_rows[None, :], 1 << 14, tickets)
    score = tickets * number_of + jnp.arange(number_of)
    return lax.top_k(score.astype(jnp.int32), top)[1].astype(jnp.int32)


def bell_draw(key, extent, deviation, most, pieces=(), kind=jnp.bfloat16):
    array = deviation * jax.random.normal(key, extent, jnp.float32)
    if pieces:
        array = array * level_of(key, extent, pieces, -0.22, 0.18)
    return jnp.clip(array, -most, most).astype(kind)


def setup_inputs(seed: int = 0) -> dict:
    key_of = jax.random.split(jax.random.key(seed), 9)
    tokens = bell_draw(key_of[0], (TOKENS, D), 1.0, 6.0, ((0, 16), (1, 2)))
    grad_out = bell_draw(key_of[1], (TOKENS, D), 1.0, 6.0, ((0, 16), (1, 2)))
    input_norm_gain = jnp.clip(1.0 + 0.18 * jax.random.normal(key_of[2], (D,), jnp.float32), 0.1, 1.9)
    q_gain = jnp.clip(1.0 + 0.18 * jax.random.normal(key_of[3], (HD,), jnp.float32), 0.1, 1.9)
    k_gain = jnp.clip(1.0 + 0.18 * jax.random.normal(key_of[4], (HD,), jnp.float32), 0.1, 1.9)
    w_qkv = bell_draw(key_of[5], (3, D, HEADS * HD), D ** -0.5, 0.078125, ((1, 16), (2, 2)))
    w_out = bell_draw(key_of[6], (HEADS * HD, D), (HEADS * HD) ** -0.5, 0.109375, ((0, 2), (1, 16)))
    pattern = distinct(key_of[7], HEADS * NQB, NQB, KSEL, 0).reshape((HEADS, NQB, KSEL))
    return {"tokens": tokens, "grad_out": grad_out, "input_norm_gain": input_norm_gain, "q_gain": q_gain, "k_gain": k_gain, "w_qkv": w_qkv, "w_out": w_out, "pattern": pattern}


def norm_rows(values, gain):
    centre = lax.optimization_barrier(jnp.mean(values, axis=-1, keepdims=True))
    centered_input = values - centre
    inverse_deviation = lax.rsqrt(lax.optimization_barrier(jnp.mean(centered_input * centered_input, axis=-1, keepdims=True)) + 1e-06)
    return centered_input * inverse_deviation * gain

def block_mask(pattern, seq_len, block):
    count = seq_len // block
    hits = pattern[:, :, :, None] == jnp.arange(count, dtype=jnp.int32)[None, None, None, :]
    allowed = jnp.any(hits, axis=2).astype(jnp.float32)
    heads = allowed.shape[0]
    spread = jnp.broadcast_to(allowed[:, :, None, :, None], (heads, count, block, count, block))
    return spread.reshape(heads, seq_len, seq_len)

def attention_grads(stacked, upstream, q_gain, k_gain, allowed):

    def attend(query, key, value):
        q_normed = norm_rows(query, q_gain)
        k_normed = norm_rows(key, k_gain)
        scores = jnp.einsum('aqhd,akhd->ahqk', q_normed, k_normed, precision=lax.Precision.HIGHEST) / math.sqrt(query.shape[-1])
        weights = jnp.exp(scores) * allowed[None]
        probs = weights / lax.optimization_barrier(jnp.sum(weights, axis=-1, keepdims=True))
        return jnp.einsum('ahqk,akhd->aqhd', probs, value, precision=lax.Precision.HIGHEST)
    widened = stacked.astype(jnp.float32)
    _, pull = jax.vjp(attend, widened[0], widened[1], widened[2])
    grads = pull(upstream.astype(jnp.float32))
    return jnp.stack(grads).astype(jnp.bfloat16)

def reference(tokens, grad_out, input_norm_gain, q_gain, k_gain, w_qkv, w_out, pattern):
    allowed = block_mask(pattern, SEQ, BLK)

    def one_image(pair):
        rows, grads = pair
        values = rows.astype(jnp.float32)
        centre = lax.optimization_barrier(jnp.mean(values, axis=-1, keepdims=True))
        centered_input = values - centre
        inverse_deviation = lax.rsqrt(lax.optimization_barrier(jnp.mean(centered_input * centered_input, axis=-1, keepdims=True)) + 1e-06)
        standardized_input = centered_input * inverse_deviation
        normalized_input = (standardized_input * input_norm_gain).astype(jnp.bfloat16)
        qkv = jnp.stack([jnp.dot(normalized_input, w_qkv[index], preferred_element_type=jnp.float32) for index in range(3)]).astype(jnp.bfloat16)
        upstream = lax.dot_general(grads, w_out, (((1,), (1,)), ((), ())), preferred_element_type=jnp.float32).astype(jnp.bfloat16)
        heads_view = qkv.reshape(3, 1, SEQ, HEADS, HD)
        d_qkv = attention_grads(heads_view, upstream.reshape(1, SEQ, HEADS, HD), q_gain, k_gain, allowed).reshape(3, SEQ, HEADS * HD)
        d_normed = jnp.zeros((SEQ, D), jnp.float32)
        for index in range(3):
            d_normed = d_normed + lax.dot_general(d_qkv[index], w_qkv[index], (((1,), (1,)), ((), ())), preferred_element_type=jnp.float32)
        normalized_gradient = d_normed * input_norm_gain
        leading_term = lax.optimization_barrier(jnp.mean(normalized_gradient, axis=-1, keepdims=True))
        trailing_term = lax.optimization_barrier(jnp.mean(normalized_gradient * standardized_input, axis=-1, keepdims=True))
        return (inverse_deviation * (normalized_gradient - leading_term - standardized_input * trailing_term)).astype(jnp.bfloat16)
    images = tokens.reshape(-1, SEQ, D)
    grad_images = grad_out.reshape(-1, SEQ, D)
    result = lax.map(one_image, (images, grad_images))
    return result.reshape(tokens.shape)
```

```python
import functools
import math

import jax
import jax.numpy as jnp
from jax import lax
from jax.experimental import pallas as pl
from jax.experimental.pallas import tpu as pltpu
from jax.sharding import PartitionSpec as P

HD = 128
SEQ = 256
BLK = 64
EPS = 1e-06


def head_grads(query, key, value, upstream, q_gain, k_gain, listed, ksel):
    scale = 1.0 / math.sqrt(HD)
    blocks = SEQ // BLK
    column_block = lax.broadcasted_iota(jnp.int32, (BLK, SEQ), 1) // BLK

    def normalize(values):
        centred = values - jnp.mean(values, axis=-1, keepdims=True)
        inverse = lax.rsqrt(jnp.mean(centred * centred, axis=-1, keepdims=True) + EPS)
        return centred * inverse, inverse

    def pull_back(grad, hat, inverse, gain):
        d_hat = grad * gain
        return inverse * (
            d_hat
            - jnp.mean(d_hat, axis=-1, keepdims=True)
            - hat * jnp.mean(d_hat * hat, axis=-1, keepdims=True)
        )

    def dot(a, b, dims, precision=None):
        return lax.dot_general(
            a, b, (dims, ((), ())), precision=precision, preferred_element_type=jnp.float32
        )

    q_hat, q_inverse = normalize(query)
    k_hat, k_inverse = normalize(key)
    q_normed = q_hat * q_gain
    k_normed = k_hat * k_gain
    scores = dot(q_normed * scale, k_normed, ((1,), (1,)), lax.Precision.HIGHEST)
    rows = []
    for i in range(blocks):
        hit = column_block == listed(i, 0)
        for s in range(1, ksel):
            hit = hit | (column_block == listed(i, s))
        rows.append(jnp.where(hit, jnp.exp(scores[i * BLK : (i + 1) * BLK]), 0.0))
    weights = jnp.concatenate(rows, axis=0)
    probs = weights / jnp.sum(weights, axis=-1, keepdims=True)
    d_probs = dot(upstream, value, ((1,), (1,)))
    d_value = dot(probs.astype(jnp.bfloat16), upstream, ((0,), (0,)))
    d_scores = probs * (d_probs - jnp.sum(probs * d_probs, axis=-1, keepdims=True))
    d_scores = (d_scores * scale).astype(jnp.bfloat16)
    d_q = dot(d_scores, k_normed.astype(jnp.bfloat16), ((1,), (0,)))
    d_k = dot(d_scores, q_normed.astype(jnp.bfloat16), ((0,), (0,)))
    return (
        pull_back(d_q, q_hat, q_inverse, q_gain).astype(jnp.bfloat16),
        pull_back(d_k, k_hat, k_inverse, k_gain).astype(jnp.bfloat16),
        d_value.astype(jnp.bfloat16),
    )


def attention_kernel(ksel, pattern_ref, q_gain_ref, k_gain_ref, qkv_ref, up_ref, out_ref):
    head = pl.program_id(1)
    blocks = SEQ // BLK
    d_q, d_k, d_v = head_grads(
        qkv_ref[:, :HD].astype(jnp.float32),
        qkv_ref[:, HD : 2 * HD].astype(jnp.float32),
        qkv_ref[:, 2 * HD :],
        up_ref[...],
        q_gain_ref[...], k_gain_ref[...],
        lambda i, s: pattern_ref[(head * blocks + i) * ksel + s],
        ksel,
    )
    out_ref[:, :HD] = d_q
    out_ref[:, HD : 2 * HD] = d_k
    out_ref[:, 2 * HD :] = d_v


def attention_grads(qkv, upstream, q_gain, k_gain, pattern):
    rows, width = upstream.shape
    heads = width // HD
    images = rows // SEQ
    return pl.pallas_call(
        functools.partial(attention_kernel, pattern.shape[2]),
        grid=(images, heads),
        out_shape=jax.ShapeDtypeStruct((rows, 3 * width), jnp.bfloat16),
        in_specs=[
            pl.BlockSpec(memory_space=pltpu.SMEM),
            pl.BlockSpec((1, HD), lambda i, h: (0, 0)),
            pl.BlockSpec((1, HD), lambda i, h: (0, 0)),
            pl.BlockSpec((SEQ, 3 * HD), lambda i, h: (i, h)),
            pl.BlockSpec((SEQ, HD), lambda i, h: (i, h)),
        ],
        out_specs=pl.BlockSpec((SEQ, 3 * HD), lambda i, h: (i, h)),
        cost_estimate=pl.CostEstimate(
            flops=images * heads * 20 * SEQ * SEQ * HD,
            bytes_accessed=rows * width * 14,
            transcendentals=images * heads * SEQ * SEQ,
        ),
    )(pattern.reshape(-1), q_gain.reshape(1, HD), k_gain.reshape(1, HD), qkv, upstream)


def piece_kernel(sizes, qkv_ref, out_ref, *piece_refs):
    start = 0
    for size, piece_ref in zip(sizes, piece_refs):
        for head in range(size):
            cols = slice((start + head) * HD, (start + head + 1) * HD)
            for part in range(3):
                lo = (3 * head + part) * HD
                piece_ref[:, lo : lo + HD] = qkv_ref[part, :, cols]
        cols = slice(start * HD, (start + size) * HD)
        piece_ref[:, 3 * size * HD :] = out_ref[cols, :].T
        start += size


def weight_pieces(w_qkv, w_out, sizes):
    depth, width = w_qkv.shape[1:]
    step = HD if depth % HD == 0 else depth
    return pl.pallas_call(
        functools.partial(piece_kernel, sizes),
        grid=(depth // step,),
        out_shape=[
            jax.ShapeDtypeStruct((depth, 4 * size * HD), w_qkv.dtype) for size in sizes
        ],
        in_specs=[
            pl.BlockSpec((3, step, width), lambda i: (0, i, 0)),
            pl.BlockSpec((width, step), lambda i: (0, i)),
        ],
        out_specs=[pl.BlockSpec((step, 4 * size * HD), lambda i: (i, 0)) for size in sizes],
        cost_estimate=pl.CostEstimate(
            flops=0, bytes_accessed=16 * depth * width, transcendentals=0
        ),
    )(w_qkv, w_out)


def projection_kernel(steps, rows_ref, grads_ref, weight_ref, qkv_ref, up_ref, qkv_sum, up_sum):
    step = pl.program_id(0)
    span = qkv_ref.shape[1]

    @pl.when(step == 0)
    def _():
        qkv_sum[...] = jnp.zeros_like(qkv_sum)
        up_sum[...] = jnp.zeros_like(up_sum)

    qkv_sum[...] += jnp.dot(
        rows_ref[...], weight_ref[:, :span], preferred_element_type=jnp.float32
    )
    up_sum[...] += jnp.dot(
        grads_ref[...], weight_ref[:, span:], preferred_element_type=jnp.float32
    )

    @pl.when(step == steps - 1)
    def _():
        qkv_ref[...] = qkv_sum[...].astype(qkv_ref.dtype)
        up_ref[...] = up_sum[...].astype(up_ref.dtype)


def project(normed, grads, weight):
    rows, depth = normed.shape
    width = weight.shape[1] // 4
    block = 1024 if depth % 1024 == 0 else depth
    steps = depth // block
    return pl.pallas_call(
        functools.partial(projection_kernel, steps),
        grid=(steps,),
        out_shape=[
            jax.ShapeDtypeStruct((rows, 3 * width), jnp.bfloat16),
            jax.ShapeDtypeStruct((rows, width), jnp.bfloat16),
        ],
        in_specs=[
            pl.BlockSpec((rows, block), lambda k: (0, k)),
            pl.BlockSpec((rows, block), lambda k: (0, k)),
            pl.BlockSpec((block, 4 * width), lambda k: (k, 0)),
        ],
        out_specs=[
            pl.BlockSpec((rows, 3 * width), lambda k: (0, 0)),
            pl.BlockSpec((rows, width), lambda k: (0, 0)),
        ],
        scratch_shapes=[
            pltpu.VMEM((rows, 3 * width), jnp.float32),
            pltpu.VMEM((rows, width), jnp.float32),
        ],
        compiler_params=pltpu.CompilerParams(vmem_limit_bytes=32 * 1024 * 1024),
        cost_estimate=pl.CostEstimate(
            flops=8 * rows * depth * width,
            bytes_accessed=8 * depth * width + 4 * rows * depth,
            transcendentals=0,
        ),
    )(normed, grads, weight)


def head_chunks(heads):
    last = max(1, heads // 4)
    return [size for size in (heads - last, last) if size > 0]


def body(tokens, grad_out, input_norm_gain, q_gain, k_gain, w_qkv, w_out, pattern):
    row_count, width = tokens.shape
    parts = lax.axis_size("tensor")
    me = lax.axis_index("tensor")
    local_heads = w_qkv.shape[2] // HD

    sizes = head_chunks(local_heads)
    pieces = weight_pieces(w_qkv, w_out, sizes)
    gathered = [lax.all_gather(piece, "dp", axis=0, tiled=True) for piece in pieces]

    def exchange(value, shift):
        return lax.ppermute(
            value, "tensor", [(source, (source + shift) % parts) for source in range(parts)]
        )

    def whole_rows(own):
        full = jnp.zeros((row_count, width * parts), own.dtype)
        full = lax.dynamic_update_slice_in_dim(full, own, me * width, 1)
        for shift in range(1, parts):
            full = lax.dynamic_update_slice_in_dim(
                full, exchange(own, shift), lax.rem(me + parts - shift, parts) * width, 1
            )
        return full

    values = whole_rows(tokens).astype(jnp.float32)
    grads_full = whole_rows(grad_out)
    centre = jnp.mean(values, axis=-1, keepdims=True)
    centred = values - centre
    inverse = lax.rsqrt(jnp.mean(centred * centred, axis=-1, keepdims=True) + EPS)
    hat = centred * inverse
    normed = (hat * input_norm_gain).astype(jnp.bfloat16)
    normed, grads_full = lax.optimization_barrier((normed, grads_full))

    def own_columns(array, index, axis):
        return lax.dynamic_slice_in_dim(array, index * width, width, axis)

    targets = [lax.rem(me + shift, parts) for shift in range(parts)]
    totals = [None] * parts
    received = []
    start = 0
    for size, weight in zip(sizes, gathered):
        span = size * HD
        last = start + size == local_heads
        if last:
            qkv, upstream = project(normed, grads_full, weight)
        else:
            qkv = jnp.dot(
                normed, weight[:, : 3 * span], preferred_element_type=jnp.float32
            ).astype(jnp.bfloat16)
            upstream = jnp.dot(
                grads_full, weight[:, 3 * span :], preferred_element_type=jnp.float32
            ).astype(jnp.bfloat16)
        d_qkv = attention_grads(
            qkv, upstream, q_gain, k_gain, pattern[start : start + size]
        )
        for shift in [*range(1, parts), 0]:
            rows = own_columns(weight, targets[shift], 0)[:, : 3 * span]
            halves = 2 if last and shift else 1
            cut = width // halves
            sums_of, arrived = [], []
            for half in range(halves):
                part = slice(half * cut, (half + 1) * cut)
                term = lax.dot_general(
                    d_qkv,
                    rows[part],
                    (((1,), (1,)), ((), ())),
                    preferred_element_type=jnp.float32,
                )
                total = term if totals[shift] is None else totals[shift][:, part] + term
                if last and shift:
                    outgoing, total, d_qkv = lax.optimization_barrier(
                        (total.astype(jnp.bfloat16), total, d_qkv)
                    )
                    arrived.append(exchange(outgoing, shift))
                sums_of.append(total)
            totals[shift] = jnp.concatenate(sums_of, axis=1) if halves > 1 else sums_of[0]
            if arrived:
                received.append(jnp.concatenate(arrived, axis=1))
        start += size
        if not last:
            normed, grads_full, totals = lax.optimization_barrier((normed, grads_full, totals))

    sums = jnp.zeros((row_count, 2), jnp.float32)
    for shift in range(parts):
        gain = own_columns(input_norm_gain, targets[shift], 0)
        scaled = totals[shift] * gain
        sums = sums + jnp.stack(
            [
                jnp.sum(scaled, axis=-1),
                jnp.sum(scaled * own_columns(hat, targets[shift], 1), axis=-1),
            ],
            axis=1,
        )
    means = sums
    for shift in range(1, parts):
        means = means + exchange(sums, shift)
    means = means / (width * parts)
    d_normed = totals[0]
    for term in received:
        d_normed = d_normed + term.astype(jnp.float32)
    d_hat = d_normed * own_columns(input_norm_gain, me, 0)
    result = inverse * (d_hat - means[:, :1] - own_columns(hat, me, 1) * means[:, 1:])
    return result.astype(jnp.bfloat16)


def fused_kernel(
    heads, ksel, pattern_ref, gain_ref, q_gain_ref, k_gain_ref, tok_hbm, grad_hbm, wqkv, wout,
    out_ref, wq_all, wo_all,
    normed, grads, tok_own, total, slot_qkv, slot_out, qkv_sum, up_sum, d_qkv,
    mean_ref, inverse_ref, x_out, x_in, z_out, z_in, x_out2, x_in2, z_out2, z_in2, sums_out, sums_in,
    local_sem, act_send, act_recv, z_send, z_recv, y_send, y_recv, c_send, c_recv, own_sem,
    load_sem, r_send, r_recv,
):
    depth = wqkv.shape[1]
    rows, half = tok_hbm.shape
    width = 2 * half
    quarter = half // 2
    me = lax.axis_index("dp")
    x = lax.axis_index("tensor")
    z = me // 4
    y = (me // 2) % 2
    c = me % 2
    p = z % 2
    planes = {0: z, 1: z + 1 - 2 * p, 2: (z + 2) % 4, 3: 3 - z}

    def block_of(plane, row, core):
        return plane * 4 + row * 2 + core

    z_peer = {k: {"dp": block_of(planes[k], y, c), "tensor": x} for k in (1, 2, 3)}
    y_peer = {"dp": block_of(z, 1 - y, c), "tensor": x}
    c_peer = {"dp": block_of(z, y, 1 - c), "tensor": x}
    x_peer = {"dp": me, "tensor": 1 - x}
    peers = [z_peer[1], z_peer[2], z_peer[3], y_peer, c_peer, x_peer]

    barrier = pltpu.get_barrier_semaphore()
    for peer in peers:
        pl.semaphore_signal(barrier, inc=1, device_id=peer, device_id_type=pl.DeviceIdType.MESH)
    pl.semaphore_wait(barrier, len(peers))

    def remote(src, dst, send, recv, peer):
        return pltpu.make_async_remote_copy(
            src_ref=src, dst_ref=dst, send_sem=send, recv_sem=recv,
            device_id=peer, device_id_type=pl.DeviceIdType.MESH,
        )

    own_rows = pl.ds(pl.multiple_of(p * rows, rows), rows)
    pair_rows = pl.ds(pl.multiple_of((1 - p) * rows, rows), rows)
    own_cols = pl.ds(pl.multiple_of(x * half, half), half)

    acts = ((tok_hbm, normed), (grad_hbm, grads))

    def act_local(i):
        return pltpu.make_async_copy(
            acts[i][0], acts[i][1].at[own_rows, own_cols], local_sem.at[i]
        )

    def act_z(i):
        return remote(
            acts[i][0], acts[i][1].at[own_rows, own_cols], act_send.at[i, 0], act_recv.at[i, 0], z_peer[1]
        )

    def act_x(i):
        return remote(
            acts[i][0], acts[i][1].at[own_rows, own_cols], act_send.at[i, 1], act_recv.at[i, 1], x_peer
        )

    def act_forward(i):
        part = acts[i][1].at[pair_rows, own_cols]
        return remote(part, part, act_send.at[i, 2], act_recv.at[i, 2], x_peer)

    def source(head, group):
        cols = pl.ds(pl.multiple_of((group * heads + head) * HD, HD), HD)
        return wqkv.at[:, :, cols], wout.at[cols, :]

    def place(head, block):
        part = pl.ds(pl.multiple_of(block * depth, depth), depth)
        return wq_all.at[head, :, part, :], wo_all.at[head, :, part]

    def z_copies(head, k):
        group = p if k == 2 else 1 - p
        return [
            remote(src, dst, z_send.at[head, k - 1, i], z_recv.at[head, k - 1, i], z_peer[k])
            for i, (src, dst) in enumerate(zip(source(head, group), place(head, me)))
        ]

    def column_part(head, k):
        if k == 0:
            return source(head, p)
        return place(head, block_of(planes[k], y, c))

    def y_copies(head, k):
        return [
            remote(src, dst, y_send.at[head, k, i], y_recv.at[head, k, i], y_peer)
            for i, (src, dst) in enumerate(
                zip(column_part(head, k), place(head, block_of(planes[k], y, c)))
            )
        ]

    def c_copies(head, k, over):
        where = place(head, block_of(planes[k], (1 - y) if over else y, c))
        src = where if over else column_part(head, k)
        return [
            remote(s, d, c_send.at[head, i], c_recv.at[head, i], c_peer)
            for i, (s, d) in enumerate(zip(src, where))
        ]

    def c_whole(head):
        whole = (
            wq_all.at[head, :, pl.ds(0, 8 * depth), :],
            wo_all.at[head, :, pl.ds(0, 8 * depth)],
        )
        return [
            remote(w, w, c_send.at[head, i], c_recv.at[head, i], c_peer) for i, w in enumerate(whole)
        ]

    def own_copies(head):
        return [
            pltpu.make_async_copy(s, d, own_sem.at[head, i])
            for i, (s, d) in enumerate(zip(source(head, p), place(head, me)))
        ]

    def start(copies):
        for copy in copies:
            copy.start()

    def send_z(head):
        for k in (2, 1, 3):
            start(z_copies(head, k))

    def forward_own(head):
        start(y_copies(head, 0))
        start(c_copies(head, 0, False))
        start(own_copies(head))

    def forward(head, k):
        for i, copy in enumerate(z_copies(head, k)):
            copy.wait_recv()
        start(y_copies(head, k))
        start(c_copies(head, k, False))

    def stage_a(head):
        forward_own(head)
        for k in (2, 1, 3):
            forward(head, k)

    def next_z(head):
        for k in (2, 1, 3):
            for copy in z_copies(head, k):
                copy.wait_send()
        @pl.when(head + 2 < heads)
        def _():
            send_z(head + 2)

    def stage_b(head):
        for k in (0, 2, 1, 3):
            for copy in y_copies(head, k):
                copy.wait_recv()
            start(c_copies(head, k, True))

    def load_copies(head, slot):
        copies = [
            pltpu.make_async_copy(
                wq_all.at[head, i], slot_qkv.at[slot, :, pl.ds(i * HD, HD)], load_sem.at[slot, i]
            )
            for i in range(3)
        ]
        copies.append(pltpu.make_async_copy(wo_all.at[head], slot_out.at[slot], load_sem.at[slot, 3]))
        return copies

    def load(head, slot):
        for copy in c_whole(head):
            copy.wait_recv()
        for copy in own_copies(head):
            copy.wait()
        start(load_copies(head, slot))

    q_gain = q_gain_ref[...]
    k_gain = k_gain_ref[...]
    scale = 1.0 / math.sqrt(HD)
    blocks = SEQ // BLK
    column_block = lax.broadcasted_iota(jnp.int32, (BLK, SEQ), 1) // BLK

    def normalize_rows():
        step = 16

        def one(i, _):
            part = pl.ds(pl.multiple_of(i * step, step), step)
            values = normed[part, :].astype(jnp.float32)
            mean = jnp.mean(values, axis=-1, keepdims=True)
            centred = values - mean
            inverse = lax.rsqrt(jnp.mean(centred * centred, axis=-1, keepdims=True) + EPS)
            mean_ref[part, :] = mean
            inverse_ref[part, :] = inverse
            normed[part, :] = (centred * inverse * gain_ref[...]).astype(jnp.bfloat16)
            return 0

        lax.fori_loop(0, 2 * rows // step, one, 0)

    def project_head(slot):
        step = 1024

        qkv_sum[...] = jnp.zeros_like(qkv_sum)
        up_sum[...] = jnp.zeros_like(up_sum)

        def one(i, _):
            part = pl.ds(pl.multiple_of(i * step, step), step)
            qkv_sum[...] += jnp.dot(
                normed[:, part], slot_qkv[slot, part, :], preferred_element_type=jnp.float32
            )
            up_sum[...] += lax.dot_general(
                grads[:, part], slot_out[slot, :, part], (((1,), (1,)), ((), ())),
                preferred_element_type=jnp.float32,
            )
            return 0

        lax.fori_loop(0, width // step, one, 0)

    def attend(head):
        def one(image, _):
            part = pl.ds(pl.multiple_of(image * SEQ, SEQ), SEQ)
            d_q, d_k, d_v = head_grads(
                qkv_sum[part, :HD].astype(jnp.bfloat16).astype(jnp.float32),
                qkv_sum[part, HD : 2 * HD].astype(jnp.bfloat16).astype(jnp.float32),
                qkv_sum[part, 2 * HD :].astype(jnp.bfloat16),
                up_sum[part, :].astype(jnp.bfloat16),
                q_gain, k_gain,
                lambda i, s: pattern_ref[((p * heads + head) * blocks + i) * ksel + s],
                ksel,
            )
            d_qkv[part, :HD] = d_q
            d_qkv[part, HD : 2 * HD] = d_k
            d_qkv[part, 2 * HD :] = d_v
            return 0

        lax.fori_loop(0, 2 * rows // SEQ, one, 0)

    def add_head(slot):
        step = 512

        def one(i, _):
            part = pl.ds(pl.multiple_of(i * step, step), step)
            total[:, part] += lax.dot_general(
                d_qkv[...], slot_qkv[slot, part, :], (((1,), (1,)), ((), ())),
                preferred_element_type=jnp.float32,
            )
            return 0

        lax.fori_loop(0, width // step, one, 0)

    early = 4
    act_z(0).start()
    act_x(0).start()
    act_z(1).start()
    act_x(1).start()
    for i in range(2):
        act_local(i).start()
    tok_copy = pltpu.make_async_copy(tok_hbm, tok_own, local_sem.at[2])
    tok_copy.start()
    send_z(0)
    send_z(1)
    total[...] = jnp.zeros_like(total)
    forward_own(0)
    for i in range(2):
        act_z(i).wait_recv()
        act_forward(i).start()

    def early_step(head, _):
        @pl.when(head > 0)
        def _():
            forward_own(head)
        for k in (2, 1, 3):
            forward(head, k)
        next_z(head)
        @pl.when(head > 0)
        def _():
            stage_b(head - 1)
        return 0

    lax.fori_loop(0, early, early_step, 0)
    load(0, 0)
    for i in range(2):
        act_local(i).wait()
        act_z(i).wait_send()
        act_x(i).wait()
        act_forward(i).wait()
    tok_copy.wait()
    normalize_rows()

    def head_step(head, _):
        slot = head % 2
        for copy in load_copies(head, slot):
            copy.wait()

        @pl.when(head + 1 < early - 1)
        def _():
            load(head + 1, 1 - slot)
        project_head(slot)
        attend(head)
        add_head(slot)

        @pl.when((head + 2 >= early) & (head + 2 < heads))
        def _():
            stage_a(head + 2)
            next_z(head + 2)

        @pl.when((head + 1 >= early - 1) & (head + 1 < heads))
        def _():
            stage_b(head + 1)
            load(head + 1, 1 - slot)
        return 0

    lax.fori_loop(0, heads, head_step, 0)

    def block_cols(which, part):
        return pl.ds(pl.multiple_of(which * half + part * quarter, quarter), quarter)

    first = [
        remote(x_out, x_in, r_send.at[0], r_recv.at[0], x_peer),
        remote(z_out, z_in, r_send.at[1], r_recv.at[1], z_peer[1]),
    ]
    second = [
        remote(z_out2, z_in2, r_send.at[2], r_recv.at[2], z_peer[1]),
        remote(x_out2, x_in2, r_send.at[3], r_recv.at[3], x_peer),
    ]
    x_out[...] = total[:, block_cols(1 - x, 0)].astype(jnp.bfloat16)
    first[0].start()
    z_out[0] = total[pair_rows, block_cols(0, 1)].astype(jnp.bfloat16)
    z_out[1] = total[pair_rows, block_cols(1, 1)].astype(jnp.bfloat16)
    first[1].start()
    first[0].wait_recv()
    z_out2[...] = (total[pair_rows, block_cols(x, 0)] + x_in[pair_rows, :].astype(jnp.float32)).astype(jnp.bfloat16)
    second[0].start()
    total[own_rows, block_cols(x, 0)] += x_in[own_rows, :].astype(jnp.float32)
    first[1].wait_recv()
    x_out2[...] = (total[own_rows, block_cols(1 - x, 1)] + z_in[1 - x].astype(jnp.float32)).astype(jnp.bfloat16)
    second[1].start()
    total[own_rows, block_cols(x, 1)] += z_in[x].astype(jnp.float32)
    second[0].wait_recv()
    total[own_rows, block_cols(x, 0)] += z_in2[...].astype(jnp.float32)
    second[1].wait_recv()
    total[own_rows, block_cols(x, 1)] += x_in2[...].astype(jnp.float32)

    step = 16
    own_gain = gain_ref[:, own_cols]
    lane = lax.broadcasted_iota(jnp.int32, (step, 128), 1)

    def parts_of(i):
        part = pl.ds(pl.multiple_of(i * step, step), step)
        shifted = pl.ds(pl.multiple_of(p * rows + i * step, step), step)
        hat = (tok_own[part, :].astype(jnp.float32) - mean_ref[shifted, :]) * inverse_ref[shifted, :]
        return part, shifted, hat, total[shifted, own_cols] * own_gain

    def sum_rows(i, _):
        part, shifted, hat, scaled = parts_of(i)
        sums_out[part, :] = jnp.where(
            lane == 0,
            jnp.sum(scaled, axis=-1, keepdims=True),
            jnp.sum(scaled * hat, axis=-1, keepdims=True),
        )
        return 0

    lax.fori_loop(0, rows // step, sum_rows, 0)
    exchange = remote(sums_out, sums_in, r_send.at[4], r_recv.at[4], x_peer)
    exchange.start()
    exchange.wait_recv()

    def finish(i, _):
        part, shifted, hat, scaled = parts_of(i)
        means = (sums_out[part, :] + sums_in[part, :]) / width
        out_ref[part, :] = (
            inverse_ref[shifted, :] * (scaled - means[:, :1] - hat * means[:, 1:2])
        ).astype(jnp.bfloat16)
        return 0

    lax.fori_loop(0, rows // step, finish, 0)

    for copy in (*first, *second, exchange):
        copy.wait_send()

    def drain(head, _):
        for k in range(4):
            for copy in y_copies(head, k):
                copy.wait_send()
        for copy in c_whole(head):
            copy.wait_send()
        return 0

    lax.fori_loop(0, heads, drain, 0)


def fused_body(tokens, grad_out, input_norm_gain, q_gain, k_gain, w_qkv, w_out, pattern):
    rows, half = tokens.shape
    depth = w_qkv.shape[1]
    width = 2 * half
    heads = w_qkv.shape[2] // HD // 2
    quarter = half // 2
    dma = pltpu.SemaphoreType.DMA
    bf16, f32 = jnp.bfloat16, jnp.float32
    vmem = pl.BlockSpec(memory_space=pltpu.VMEM)
    hbm = pl.BlockSpec(memory_space=pl.ANY)
    return pl.pallas_call(
        functools.partial(fused_kernel, heads, pattern.shape[2]),
        out_shape=[
            jax.ShapeDtypeStruct((rows, half), bf16),
            jax.ShapeDtypeStruct((heads, 3, width, HD), bf16),
            jax.ShapeDtypeStruct((heads, HD, width), bf16),
        ],
        in_specs=[pl.BlockSpec(memory_space=pltpu.SMEM), vmem, vmem, vmem, hbm, hbm, hbm, hbm],
        out_specs=[vmem, hbm, hbm],
        scratch_shapes=[
            pltpu.VMEM((2 * rows, width), bf16),
            pltpu.VMEM((2 * rows, width), bf16),
            pltpu.VMEM((rows, half), bf16),
            pltpu.VMEM((2 * rows, width), f32),
            pltpu.VMEM((2, width, 3 * HD), bf16),
            pltpu.VMEM((2, HD, width), bf16),
            pltpu.VMEM((2 * rows, 3 * HD), f32),
            pltpu.VMEM((2 * rows, HD), f32),
            pltpu.VMEM((2 * rows, 3 * HD), bf16),
            pltpu.VMEM((2 * rows, 1), f32),
            pltpu.VMEM((2 * rows, 1), f32),
            pltpu.VMEM((2 * rows, quarter), bf16),
            pltpu.VMEM((2 * rows, quarter), bf16),
            pltpu.VMEM((2, rows, quarter), bf16),
            pltpu.VMEM((2, rows, quarter), bf16),
            pltpu.VMEM((rows, quarter), bf16),
            pltpu.VMEM((rows, quarter), bf16),
            pltpu.VMEM((rows, quarter), bf16),
            pltpu.VMEM((rows, quarter), bf16),
            pltpu.VMEM((rows, 128), f32),
            pltpu.VMEM((rows, 128), f32),
            dma((3,)),
            dma((2, 3)),
            dma((2, 3)),
            dma((heads, 3, 2)),
            dma((heads, 3, 2)),
            dma((heads, 4, 2)),
            dma((heads, 4, 2)),
            dma((heads, 2)),
            dma((heads, 2)),
            dma((heads, 2)),
            dma((2, 4)),
            dma((5,)),
            dma((5,)),
        ],
        compiler_params=pltpu.CompilerParams(
            collective_id=0, has_side_effects=True, vmem_limit_bytes=60 * 1024 * 1024
        ),
        cost_estimate=pl.CostEstimate(
            flops=14 * 2 * rows * width * heads * HD,
            bytes_accessed=16 * width * heads * HD,
            transcendentals=2 * rows * heads * SEQ,
        ),
        name="fused",
    )(
        pattern.reshape(-1), input_norm_gain.reshape(1, width), q_gain.reshape(1, HD),
        k_gain.reshape(1, HD), tokens, grad_out, w_qkv, w_out,
    )[0]


def solution(mesh):
    fits = mesh.shape["dp"] == 16 and mesh.shape["tensor"] == 2
    return jax.shard_map(
        fused_body if fits else body,
        mesh=mesh,
        in_specs=(
            P("dp", "tensor"),
            P("dp", "tensor"),
            P(),
            P(),
            P(),
            P(None, "dp", "tensor"),
            P("tensor", "dp"),
            P("tensor", None, None),
        ),
        out_specs=P("dp", "tensor"),
        check_vma=False,
    )
```

```python
import functools
import math

import jax
import jax.numpy as jnp
from jax import lax
from jax.experimental import pallas as pl
from jax.experimental.pallas import tpu as pltpu
from jax.sharding import PartitionSpec as P

HD = 128
SEQ = 256
BLK = 64
EPS = 1e-06


def head_grads(query, key, value, upstream, q_gain, k_gain, listed, ksel):
    scale = 1.0 / math.sqrt(HD)
    blocks = SEQ // BLK
    column_block = lax.broadcasted_iota(jnp.int32, (BLK, SEQ), 1) // BLK

    def normalize(values):
        centred = values - jnp.mean(values, axis=-1, keepdims=True)
        inverse = lax.rsqrt(jnp.mean(centred * centred, axis=-1, keepdims=True) + EPS)
        return centred * inverse, inverse

    def pull_back(grad, hat, inverse, gain):
        d_hat = grad * gain
        return inverse * (
            d_hat
            - jnp.mean(d_hat, axis=-1, keepdims=True)
            - hat * jnp.mean(d_hat * hat, axis=-1, keepdims=True)
        )

    def dot(a, b, dims, precision=None):
        return lax.dot_general(
            a, b, (dims, ((), ())), precision=precision, preferred_element_type=jnp.float32
        )

    q_hat, q_inverse = normalize(query)
    k_hat, k_inverse = normalize(key)
    q_normed = q_hat * q_gain
    k_normed = k_hat * k_gain
    scores = dot(q_normed * scale, k_normed, ((1,), (1,)), lax.Precision.HIGHEST)
    rows = []
    for i in range(blocks):
        hit = column_block == listed(i, 0)
        for s in range(1, ksel):
            hit = hit | (column_block == listed(i, s))
        rows.append(jnp.where(hit, jnp.exp(scores[i * BLK : (i + 1) * BLK]), 0.0))
    weights = jnp.concatenate(rows, axis=0)
    probs = weights / jnp.sum(weights, axis=-1, keepdims=True)
    d_probs = dot(upstream, value, ((1,), (1,)))
    d_value = dot(probs.astype(jnp.bfloat16), upstream, ((0,), (0,)))
    d_scores = probs * (d_probs - jnp.sum(probs * d_probs, axis=-1, keepdims=True))
    d_scores = (d_scores * scale).astype(jnp.bfloat16)
    d_q = dot(d_scores, k_normed.astype(jnp.bfloat16), ((1,), (0,)))
    d_k = dot(d_scores, q_normed.astype(jnp.bfloat16), ((0,), (0,)))
    return (
        pull_back(d_q, q_hat, q_inverse, q_gain).astype(jnp.bfloat16),
        pull_back(d_k, k_hat, k_inverse, k_gain).astype(jnp.bfloat16),
        d_value.astype(jnp.bfloat16),
    )


def attention_kernel(ksel, pattern_ref, q_gain_ref, k_gain_ref, qkv_ref, up_ref, out_ref):
    head = pl.program_id(1)
    blocks = SEQ // BLK
    d_q, d_k, d_v = head_grads(
        qkv_ref[:, :HD].astype(jnp.float32),
        qkv_ref[:, HD : 2 * HD].astype(jnp.float32),
        qkv_ref[:, 2 * HD :],
        up_ref[...],
        q_gain_ref[...], k_gain_ref[...],
        lambda i, s: pattern_ref[(head * blocks + i) * ksel + s],
        ksel,
    )
    out_ref[:, :HD] = d_q
    out_ref[:, HD : 2 * HD] = d_k
    out_ref[:, 2 * HD :] = d_v


def attention_grads(qkv, upstream, q_gain, k_gain, pattern):
    rows, width = upstream.shape
    heads = width // HD
    images = rows // SEQ
    return pl.pallas_call(
        functools.partial(attention_kernel, pattern.shape[2]),
        grid=(images, heads),
        out_shape=jax.ShapeDtypeStruct((rows, 3 * width), jnp.bfloat16),
        in_specs=[
            pl.BlockSpec(memory_space=pltpu.SMEM),
            pl.BlockSpec((1, HD), lambda i, h: (0, 0)),
            pl.BlockSpec((1, HD), lambda i, h: (0, 0)),
            pl.BlockSpec((SEQ, 3 * HD), lambda i, h: (i, h)),
            pl.BlockSpec((SEQ, HD), lambda i, h: (i, h)),
        ],
        out_specs=pl.BlockSpec((SEQ, 3 * HD), lambda i, h: (i, h)),
        cost_estimate=pl.CostEstimate(
            flops=images * heads * 20 * SEQ * SEQ * HD,
            bytes_accessed=rows * width * 14,
            transcendentals=images * heads * SEQ * SEQ,
        ),
    )(pattern.reshape(-1), q_gain.reshape(1, HD), k_gain.reshape(1, HD), qkv, upstream)


def piece_kernel(sizes, qkv_ref, out_ref, *piece_refs):
    start = 0
    for size, piece_ref in zip(sizes, piece_refs):
        for head in range(size):
            cols = slice((start + head) * HD, (start + head + 1) * HD)
            for part in range(3):
                lo = (3 * head + part) * HD
                piece_ref[:, lo : lo + HD] = qkv_ref[part, :, cols]
        cols = slice(start * HD, (start + size) * HD)
        piece_ref[:, 3 * size * HD :] = out_ref[cols, :].T
        start += size


def weight_pieces(w_qkv, w_out, sizes):
    depth, width = w_qkv.shape[1:]
    step = HD if depth % HD == 0 else depth
    return pl.pallas_call(
        functools.partial(piece_kernel, sizes),
        grid=(depth // step,),
        out_shape=[
            jax.ShapeDtypeStruct((depth, 4 * size * HD), w_qkv.dtype) for size in sizes
        ],
        in_specs=[
            pl.BlockSpec((3, step, width), lambda i: (0, i, 0)),
            pl.BlockSpec((width, step), lambda i: (0, i)),
        ],
        out_specs=[pl.BlockSpec((step, 4 * size * HD), lambda i: (i, 0)) for size in sizes],
        cost_estimate=pl.CostEstimate(
            flops=0, bytes_accessed=16 * depth * width, transcendentals=0
        ),
    )(w_qkv, w_out)


def projection_kernel(steps, rows_ref, grads_ref, weight_ref, qkv_ref, up_ref, qkv_sum, up_sum):
    step = pl.program_id(0)
    span = qkv_ref.shape[1]

    @pl.when(step == 0)
    def _():
        qkv_sum[...] = jnp.zeros_like(qkv_sum)
        up_sum[...] = jnp.zeros_like(up_sum)

    qkv_sum[...] += jnp.dot(
        rows_ref[...], weight_ref[:, :span], preferred_element_type=jnp.float32
    )
    up_sum[...] += jnp.dot(
        grads_ref[...], weight_ref[:, span:], preferred_element_type=jnp.float32
    )

    @pl.when(step == steps - 1)
    def _():
        qkv_ref[...] = qkv_sum[...].astype(qkv_ref.dtype)
        up_ref[...] = up_sum[...].astype(up_ref.dtype)


def project(normed, grads, weight):
    rows, depth = normed.shape
    width = weight.shape[1] // 4
    block = 1024 if depth % 1024 == 0 else depth
    steps = depth // block
    return pl.pallas_call(
        functools.partial(projection_kernel, steps),
        grid=(steps,),
        out_shape=[
            jax.ShapeDtypeStruct((rows, 3 * width), jnp.bfloat16),
            jax.ShapeDtypeStruct((rows, width), jnp.bfloat16),
        ],
        in_specs=[
            pl.BlockSpec((rows, block), lambda k: (0, k)),
            pl.BlockSpec((rows, block), lambda k: (0, k)),
            pl.BlockSpec((block, 4 * width), lambda k: (k, 0)),
        ],
        out_specs=[
            pl.BlockSpec((rows, 3 * width), lambda k: (0, 0)),
            pl.BlockSpec((rows, width), lambda k: (0, 0)),
        ],
        scratch_shapes=[
            pltpu.VMEM((rows, 3 * width), jnp.float32),
            pltpu.VMEM((rows, width), jnp.float32),
        ],
        compiler_params=pltpu.CompilerParams(vmem_limit_bytes=32 * 1024 * 1024),
        cost_estimate=pl.CostEstimate(
            flops=8 * rows * depth * width,
            bytes_accessed=8 * depth * width + 4 * rows * depth,
            transcendentals=0,
        ),
    )(normed, grads, weight)


def head_chunks(heads):
    last = max(1, heads // 4)
    return [size for size in (heads - last, last) if size > 0]


def body(tokens, grad_out, input_norm_gain, q_gain, k_gain, w_qkv, w_out, pattern):
    row_count, width = tokens.shape
    parts = lax.axis_size("tensor")
    me = lax.axis_index("tensor")
    local_heads = w_qkv.shape[2] // HD

    sizes = head_chunks(local_heads)
    pieces = weight_pieces(w_qkv, w_out, sizes)
    gathered = [lax.all_gather(piece, "dp", axis=0, tiled=True) for piece in pieces]

    def exchange(value, shift):
        return lax.ppermute(
            value, "tensor", [(source, (source + shift) % parts) for source in range(parts)]
        )

    def whole_rows(own):
        full = jnp.zeros((row_count, width * parts), own.dtype)
        full = lax.dynamic_update_slice_in_dim(full, own, me * width, 1)
        for shift in range(1, parts):
            full = lax.dynamic_update_slice_in_dim(
                full, exchange(own, shift), lax.rem(me + parts - shift, parts) * width, 1
            )
        return full

    values = whole_rows(tokens).astype(jnp.float32)
    grads_full = whole_rows(grad_out)
    centre = jnp.mean(values, axis=-1, keepdims=True)
    centred = values - centre
    inverse = lax.rsqrt(jnp.mean(centred * centred, axis=-1, keepdims=True) + EPS)
    hat = centred * inverse
    normed = (hat * input_norm_gain).astype(jnp.bfloat16)
    normed, grads_full = lax.optimization_barrier((normed, grads_full))

    def own_columns(array, index, axis):
        return lax.dynamic_slice_in_dim(array, index * width, width, axis)

    targets = [lax.rem(me + shift, parts) for shift in range(parts)]
    totals = [None] * parts
    received = []
    start = 0
    for size, weight in zip(sizes, gathered):
        span = size * HD
        last = start + size == local_heads
        if last:
            qkv, upstream = project(normed, grads_full, weight)
        else:
            qkv = jnp.dot(
                normed, weight[:, : 3 * span], preferred_element_type=jnp.float32
            ).astype(jnp.bfloat16)
            upstream = jnp.dot(
                grads_full, weight[:, 3 * span :], preferred_element_type=jnp.float32
            ).astype(jnp.bfloat16)
        d_qkv = attention_grads(
            qkv, upstream, q_gain, k_gain, pattern[start : start + size]
        )
        for shift in [*range(1, parts), 0]:
            rows = own_columns(weight, targets[shift], 0)[:, : 3 * span]
            halves = 2 if last and shift else 1
            cut = width // halves
            sums_of, arrived = [], []
            for half in range(halves):
                part = slice(half * cut, (half + 1) * cut)
                term = lax.dot_general(
                    d_qkv,
                    rows[part],
                    (((1,), (1,)), ((), ())),
                    preferred_element_type=jnp.float32,
                )
                total = term if totals[shift] is None else totals[shift][:, part] + term
                if last and shift:
                    outgoing, total, d_qkv = lax.optimization_barrier(
                        (total.astype(jnp.bfloat16), total, d_qkv)
                    )
                    arrived.append(exchange(outgoing, shift))
                sums_of.append(total)
            totals[shift] = jnp.concatenate(sums_of, axis=1) if halves > 1 else sums_of[0]
            if arrived:
                received.append(jnp.concatenate(arrived, axis=1))
        start += size
        if not last:
            normed, grads_full, totals = lax.optimization_barrier((normed, grads_full, totals))

    sums = jnp.zeros((row_count, 2), jnp.float32)
    for shift in range(parts):
        gain = own_columns(input_norm_gain, targets[shift], 0)
        scaled = totals[shift] * gain
        sums = sums + jnp.stack(
            [
                jnp.sum(scaled, axis=-1),
                jnp.sum(scaled * own_columns(hat, targets[shift], 1), axis=-1),
            ],
            axis=1,
        )
    means = sums
    for shift in range(1, parts):
        means = means + exchange(sums, shift)
    means = means / (width * parts)
    d_normed = totals[0]
    for term in received:
        d_normed = d_normed + term.astype(jnp.float32)
    d_hat = d_normed * own_columns(input_norm_gain, me, 0)
    result = inverse * (d_hat - means[:, :1] - own_columns(hat, me, 1) * means[:, 1:])
    return result.astype(jnp.bfloat16)


CUTS = 4


def fused_kernel(
    heads, ksel, pattern_ref, gain_ref, q_gain_ref, k_gain_ref, tok_hbm, grad_hbm, wqkv, wout,
    out_ref, wq_all, wo_all,
    normed, grads, tok_own, total, slot_qkv, slot_out, qkv_sum, up_sum, d_qkv,
    mean_ref, inverse_ref, x_out, x_in, z_out, z_in, x_out2, x_in2, z_out2, z_in2, sums_out, sums_in,
    local_sem, act_send, act_recv, z_send, z_recv, y_send, y_recv, c_send, c_recv, own_sem,
    load_sem, r_send, r_recv,
):
    depth = wqkv.shape[1]
    rows, half = tok_hbm.shape
    width = 2 * half
    quarter = half // 2
    me = lax.axis_index("dp")
    x = lax.axis_index("tensor")
    z = me // 4
    y = (me // 2) % 2
    c = me % 2
    p = z % 2
    inner = (z == 1) | (z == 2)
    window = CUTS
    units = heads * CUTS
    planes = {0: z, 1: z + 1 - 2 * p, 2: (z + 2) % 4, 3: 3 - z}

    def block_of(plane, row, core):
        return plane * 4 + row * 2 + core

    z_peer = {k: {"dp": block_of(planes[k], y, c), "tensor": x} for k in (1, 2, 3)}
    y_peer = {"dp": block_of(z, 1 - y, c), "tensor": x}
    c_peer = {"dp": block_of(z, y, 1 - c), "tensor": x}
    x_peer = {"dp": me, "tensor": 1 - x}
    peers = [z_peer[1], z_peer[2], z_peer[3], y_peer, c_peer, x_peer]

    barrier = pltpu.get_barrier_semaphore()
    for peer in peers:
        pl.semaphore_signal(barrier, inc=1, device_id=peer, device_id_type=pl.DeviceIdType.MESH)
    pl.semaphore_wait(barrier, len(peers))

    def remote(src, dst, send, recv, peer):
        return pltpu.make_async_remote_copy(
            src_ref=src, dst_ref=dst, send_sem=send, recv_sem=recv,
            device_id=peer, device_id_type=pl.DeviceIdType.MESH,
        )

    own_rows = pl.ds(pl.multiple_of(p * rows, rows), rows)
    pair_rows = pl.ds(pl.multiple_of((1 - p) * rows, rows), rows)
    own_cols = pl.ds(pl.multiple_of(x * half, half), half)

    acts = ((tok_hbm, normed), (grad_hbm, grads))

    def act_local(i):
        return pltpu.make_async_copy(
            acts[i][0], acts[i][1].at[own_rows, own_cols], local_sem.at[i]
        )

    def act_z(i):
        return remote(
            acts[i][0], acts[i][1].at[own_rows, own_cols], act_send.at[i, 0], act_recv.at[i, 0], z_peer[1]
        )

    def act_x(i):
        return remote(
            acts[i][0], acts[i][1].at[own_rows, own_cols], act_send.at[i, 1], act_recv.at[i, 1], x_peer
        )

    def act_forward(i):
        part = acts[i][1].at[pair_rows, own_cols]
        return remote(part, part, act_send.at[i, 2], act_recv.at[i, 2], x_peer)

    cut = depth // CUTS
    cut_out = HD // CUTS

    def source(unit, group):
        head, part = unit // CUTS, unit % CUTS
        column = (group * heads + head) * HD
        rows_out = pl.ds(pl.multiple_of(column + part * cut_out, cut_out), cut_out)
        return (
            wqkv.at[:, pl.ds(pl.multiple_of(part * cut, cut), cut), pl.ds(pl.multiple_of(column, HD), HD)],
            wout.at[rows_out, :],
        )

    def place(unit, block):
        head, part = unit // CUTS, unit % CUTS
        at = pl.ds(pl.multiple_of(block * depth + part * cut, cut), cut)
        return (
            wq_all.at[head, :, at, :],
            wo_all.at[
                head,
                pl.ds(pl.multiple_of(part * cut_out, cut_out), cut_out),
                pl.ds(pl.multiple_of(block * depth, depth), depth),
            ],
        )

    def z_copies(unit, k):
        group = p if k == 2 else 1 - p
        return [
            remote(src, dst, z_send.at[unit, k - 1, i], z_recv.at[unit, k - 1, i], z_peer[k])
            for i, (src, dst) in enumerate(zip(source(unit, group), place(unit, me)))
        ]

    def column_part(unit, k):
        if k == 0:
            return source(unit, p)
        return place(unit, block_of(planes[k], y, c))

    def y_copies(unit, k):
        return [
            remote(src, dst, y_send.at[unit, k, i], y_recv.at[unit, k, i], y_peer)
            for i, (src, dst) in enumerate(
                zip(column_part(unit, k), place(unit, block_of(planes[k], y, c)))
            )
        ]

    def c_copies(unit, k, over):
        where = place(unit, block_of(planes[k], (1 - y) if over else y, c))
        src = where if over else column_part(unit, k)
        head = unit // CUTS
        return [
            remote(s, d, c_send.at[head, i], c_recv.at[head, i], c_peer)
            for i, (s, d) in enumerate(zip(src, where))
        ]

    def c_whole(head):
        whole = (
            wq_all.at[head, :, pl.ds(0, 8 * depth), :],
            wo_all.at[head, :, pl.ds(0, 8 * depth)],
        )
        return [
            remote(w, w, c_send.at[head, i], c_recv.at[head, i], c_peer) for i, w in enumerate(whole)
        ]

    def own_copies(head, back):
        part = pl.ds(pl.multiple_of(head * depth, depth), depth)
        cols = pl.ds(pl.multiple_of((p * heads + head) * HD, HD), HD)
        mine = pl.ds(pl.multiple_of(me * depth, depth), depth)
        legs = [
            (
                wqkv.at[i, :, cols],
                slot_qkv.at[part, pl.ds(i * HD, HD)],
                wq_all.at[head, i, mine, :],
            )
            for i in range(3)
        ]
        legs.append((wout.at[cols, :], slot_out.at[:HD, part], wo_all.at[head, :, mine]))
        return [
            pltpu.make_async_copy(*((mid, last) if back else (first, mid)), own_sem.at[head, i])
            for i, (first, mid, last) in enumerate(legs)
        ]

    def start(copies):
        for copy in copies:
            copy.start()

    def forward_own(unit):
        start(y_copies(unit, 0))
        start(c_copies(unit, 0, False))

    def forward(unit, k):
        for copy in z_copies(unit, k):
            copy.wait_recv()
        start(y_copies(unit, k))
        start(c_copies(unit, k, False))

    def advance(unit, k):
        forward(unit, k)
        for copy in z_copies(unit, k):
            copy.wait_send()

        @pl.when(unit + window < units)
        def _():
            start(z_copies(unit + window, k))

    def stage_a(unit):
        for k in (1, 2):
            advance(unit, k)

        @pl.when(jnp.logical_not(inner))
        def _():
            advance(unit, 3)

    def stage_b(unit):
        for k in (0, 3, 1, 2):
            for copy in y_copies(unit, k):
                copy.wait_recv()
            start(c_copies(unit, k, True))

    def load_copies(head):
        pos = head % 2
        copies = [
            pltpu.make_async_copy(
                wq_all.at[head, i],
                slot_qkv.at[:, pl.ds(pl.multiple_of((pos * 3 + i) * HD, HD), HD)],
                load_sem.at[pos, i],
            )
            for i in range(3)
        ]
        copies.append(
            pltpu.make_async_copy(
                wo_all.at[head],
                slot_out.at[pl.ds(pl.multiple_of(pos * HD, HD), HD), :],
                load_sem.at[pos, 3],
            )
        )
        return copies

    def load(head):
        for copy in c_whole(head):
            copy.wait_recv()
        start(load_copies(head))

    def loaded(head):
        for copy in load_copies(head):
            copy.wait()

    q_gain = q_gain_ref[...]
    k_gain = k_gain_ref[...]
    blocks = SEQ // BLK

    def normalize_rows(half_of):
        step = 16

        def one(i, _):
            part = pl.ds(pl.multiple_of(half_of * rows + i * step, step), step)
            values = normed[part, :].astype(jnp.float32)
            mean = jnp.mean(values, axis=-1, keepdims=True)
            centred = values - mean
            inverse = lax.rsqrt(jnp.mean(centred * centred, axis=-1, keepdims=True) + EPS)
            mean_ref[part, :] = mean
            inverse_ref[part, :] = inverse
            normed[part, :] = (centred * inverse * gain_ref[...]).astype(jnp.bfloat16)
            return 0

        lax.fori_loop(0, rows // step, one, 0)

    def project_pair():
        step = 1024
        qkv_sum[...] = jnp.zeros_like(qkv_sum)
        up_sum[...] = jnp.zeros_like(up_sum)

        def one(i, _):
            part = pl.ds(pl.multiple_of(i * step, step), step)
            qkv_sum[...] += jnp.dot(
                normed[:, part], slot_qkv[part, :], preferred_element_type=jnp.float32
            )
            up_sum[...] += lax.dot_general(
                grads[:, part], slot_out[:, part], (((1,), (1,)), ((), ())),
                preferred_element_type=jnp.float32,
            )
            return 0

        lax.fori_loop(0, width // step, one, 0)

    def attend_pair(pair):
        images = 2 * rows // SEQ

        def one(i, _):
            which = i // images
            part = pl.ds(pl.multiple_of((i % images) * SEQ, SEQ), SEQ)
            cols = [pl.ds(pl.multiple_of((which * 3 + j) * HD, HD), HD) for j in range(3)]
            up_cols = pl.ds(pl.multiple_of(which * HD, HD), HD)
            results = head_grads(
                qkv_sum[part, cols[0]].astype(jnp.bfloat16).astype(jnp.float32),
                qkv_sum[part, cols[1]].astype(jnp.bfloat16).astype(jnp.float32),
                qkv_sum[part, cols[2]].astype(jnp.bfloat16),
                up_sum[part, up_cols].astype(jnp.bfloat16),
                q_gain, k_gain,
                lambda i, s: pattern_ref[((p * heads + 2 * pair + which) * blocks + i) * ksel + s],
                ksel,
            )
            for j in range(3):
                d_qkv[part, cols[j]] = results[j]
            return 0

        lax.fori_loop(0, 2 * images, one, 0)

    def add_cols(which, part_of):
        step = 512
        base = which * half + part_of * quarter

        def one(i, _):
            part = pl.ds(pl.multiple_of(base + i * step, step), step)
            total[:, part] += lax.dot_general(
                d_qkv[...], slot_qkv[part, :], (((1,), (1,)), ((), ())),
                preferred_element_type=jnp.float32,
            )
            return 0

        lax.fori_loop(0, quarter // step, one, 0)

    for i in range(2):
        act_z(i).start()
        act_x(i).start()

    def each_head(act, low=0, high=heads):
        def one(head, _):
            act(head)
            return 0

        lax.fori_loop(low, high, one, 0)

    @pl.when(inner)
    def _():
        each_head(lambda unit: start(z_copies(unit, 3)), 0, units)

    each_head(forward_own, 0, units)
    each_head(lambda head: start(own_copies(head, False)))
    for i in range(2):
        act_local(i).start()
    tok_copy = pltpu.make_async_copy(tok_hbm, tok_own, local_sem.at[2])
    tok_copy.start()
    total[...] = jnp.zeros_like(total)

    def turn_own(head):
        for copy in own_copies(head, False):
            copy.wait()
        start(own_copies(head, True))

    each_head(turn_own)

    @pl.when(inner)
    def _():
        each_head(lambda unit: forward(unit, 3), 0, units // 2)

    act_z(0).wait_recv()
    act_forward(0).start()

    @pl.when(inner)
    def _():
        each_head(lambda unit: forward(unit, 3), units // 2, units)

    act_z(1).wait_recv()
    act_forward(1).start()
    for i in range(2):
        act_z(i).wait_send()

    def first_units(unit):
        for k in (1, 2):
            start(z_copies(unit, k))

        @pl.when(jnp.logical_not(inner))
        def _():
            start(z_copies(unit, 3))

    each_head(first_units, 0, window)

    def wait_own(head):
        for copy in own_copies(head, True):
            copy.wait()

    each_head(wait_own)

    begin = heads // 2 * CUTS

    def unit_step(unit):
        stage_a(unit)

        @pl.when(unit > 0)
        def _():
            stage_b(unit - 1)

        at = unit - begin

        @pl.when(at == 0)
        def _():
            load(0)
            load(1)
            for i in range(2):
                act_local(i).wait()
                act_x(i).wait()
                act_forward(i).wait()

        @pl.when((at >= 0) & (at < 2))
        def _():
            normalize_rows(at)

        @pl.when((at == 2) | (at == 6))
        def _():
            pair = (at - 2) // 4
            loaded(2 * pair)
            loaded(2 * pair + 1)
            project_pair()

        @pl.when((at == 3) | (at == 7))
        def _():
            attend_pair((at - 3) // 4)

        @pl.when((at == 4) | (at == 8))
        def _():
            for which in range(2):
                for part_of in range(2):
                    add_cols(which, part_of)

        @pl.when(at == 4)
        def _():
            load(2)
            load(3)

        @pl.when(at == 8)
        def _():
            load(4)

    each_head(unit_step, 0, units)
    tok_copy.wait()
    stage_b(units - 1)
    load(5)
    loaded(4)
    loaded(5)
    project_pair()
    attend_pair(2)

    def block_cols(which, part):
        return pl.ds(pl.multiple_of(which * half + part * quarter, quarter), quarter)

    first = [
        remote(x_out, x_in, r_send.at[0], r_recv.at[0], x_peer),
        remote(z_out, z_in, r_send.at[1], r_recv.at[1], z_peer[1]),
    ]
    second = [
        remote(z_out2, z_in2, r_send.at[2], r_recv.at[2], z_peer[1]),
        remote(x_out2, x_in2, r_send.at[3], r_recv.at[3], x_peer),
    ]
    add_cols(1 - x, 0)
    x_out[...] = total[:, block_cols(1 - x, 0)].astype(jnp.bfloat16)
    first[0].start()
    add_cols(0, 1)
    add_cols(1, 1)
    z_out[0] = total[pair_rows, block_cols(0, 1)].astype(jnp.bfloat16)
    z_out[1] = total[pair_rows, block_cols(1, 1)].astype(jnp.bfloat16)
    first[1].start()
    add_cols(x, 0)
    first[0].wait_recv()
    z_out2[...] = (total[pair_rows, block_cols(x, 0)] + x_in[pair_rows, :].astype(jnp.float32)).astype(jnp.bfloat16)
    second[0].start()
    total[own_rows, block_cols(x, 0)] += x_in[own_rows, :].astype(jnp.float32)
    first[1].wait_recv()
    x_out2[...] = (total[own_rows, block_cols(1 - x, 1)] + z_in[1 - x].astype(jnp.float32)).astype(jnp.bfloat16)
    second[1].start()
    total[own_rows, block_cols(x, 1)] += z_in[x].astype(jnp.float32)
    second[0].wait_recv()
    total[own_rows, block_cols(x, 0)] += z_in2[...].astype(jnp.float32)
    second[1].wait_recv()
    total[own_rows, block_cols(x, 1)] += x_in2[...].astype(jnp.float32)

    step = 16
    own_gain = gain_ref[:, own_cols]
    lane = lax.broadcasted_iota(jnp.int32, (step, 128), 1)

    def parts_of(i):
        part = pl.ds(pl.multiple_of(i * step, step), step)
        shifted = pl.ds(pl.multiple_of(p * rows + i * step, step), step)
        hat = (tok_own[part, :].astype(jnp.float32) - mean_ref[shifted, :]) * inverse_ref[shifted, :]
        return part, shifted, hat, total[shifted, own_cols] * own_gain

    def sum_rows(i, _):
        part, shifted, hat, scaled = parts_of(i)
        sums_out[part, :] = jnp.where(
            lane == 0,
            jnp.sum(scaled, axis=-1, keepdims=True),
            jnp.sum(scaled * hat, axis=-1, keepdims=True),
        )
        return 0

    lax.fori_loop(0, rows // step, sum_rows, 0)
    exchange = remote(sums_out, sums_in, r_send.at[4], r_recv.at[4], x_peer)
    exchange.start()
    exchange.wait_recv()

    def finish(i, _):
        part, shifted, hat, scaled = parts_of(i)
        means = (sums_out[part, :] + sums_in[part, :]) / width
        out_ref[part, :] = (
            inverse_ref[shifted, :] * (scaled - means[:, :1] - hat * means[:, 1:2])
        ).astype(jnp.bfloat16)
        return 0

    lax.fori_loop(0, rows // step, finish, 0)

    for copy in (*first, *second, exchange):
        copy.wait_send()

    def drain(unit):
        @pl.when(inner)
        def _():
            for copy in z_copies(unit, 3):
                copy.wait_send()

        for k in range(4):
            for copy in y_copies(unit, k):
                copy.wait_send()

    each_head(drain, 0, units)

    def drain_core(head):
        for copy in c_whole(head):
            copy.wait_send()

    each_head(drain_core)


def fused_body(tokens, grad_out, input_norm_gain, q_gain, k_gain, w_qkv, w_out, pattern):
    rows, half = tokens.shape
    depth = w_qkv.shape[1]
    width = 2 * half
    heads = w_qkv.shape[2] // HD // 2
    quarter = half // 2
    dma = pltpu.SemaphoreType.DMA
    bf16, f32 = jnp.bfloat16, jnp.float32
    vmem = pl.BlockSpec(memory_space=pltpu.VMEM)
    hbm = pl.BlockSpec(memory_space=pl.ANY)
    return pl.pallas_call(
        functools.partial(fused_kernel, heads, pattern.shape[2]),
        out_shape=[
            jax.ShapeDtypeStruct((rows, half), bf16),
            jax.ShapeDtypeStruct((heads, 3, width, HD), bf16),
            jax.ShapeDtypeStruct((heads, HD, width), bf16),
        ],
        in_specs=[pl.BlockSpec(memory_space=pltpu.SMEM), vmem, vmem, vmem, hbm, hbm, hbm, hbm],
        out_specs=[vmem, hbm, hbm],
        scratch_shapes=[
            pltpu.VMEM((2 * rows, width), bf16),
            pltpu.VMEM((2 * rows, width), bf16),
            pltpu.VMEM((rows, half), bf16),
            pltpu.VMEM((2 * rows, width), f32),
            pltpu.VMEM((width, 6 * HD), bf16),
            pltpu.VMEM((2 * HD, width), bf16),
            pltpu.VMEM((2 * rows, 6 * HD), f32),
            pltpu.VMEM((2 * rows, 2 * HD), f32),
            pltpu.VMEM((2 * rows, 6 * HD), bf16),
            pltpu.VMEM((2 * rows, 1), f32),
            pltpu.VMEM((2 * rows, 1), f32),
            pltpu.VMEM((2 * rows, quarter), bf16),
            pltpu.VMEM((2 * rows, quarter), bf16),
            pltpu.VMEM((2, rows, quarter), bf16),
            pltpu.VMEM((2, rows, quarter), bf16),
            pltpu.VMEM((rows, quarter), bf16),
            pltpu.VMEM((rows, quarter), bf16),
            pltpu.VMEM((rows, quarter), bf16),
            pltpu.VMEM((rows, quarter), bf16),
            pltpu.VMEM((rows, 128), f32),
            pltpu.VMEM((rows, 128), f32),
            dma((3,)),
            dma((2, 3)),
            dma((2, 3)),
            dma((heads * CUTS, 3, 2)),
            dma((heads * CUTS, 3, 2)),
            dma((heads * CUTS, 4, 2)),
            dma((heads * CUTS, 4, 2)),
            dma((heads, 2)),
            dma((heads, 2)),
            dma((heads, 4)),
            dma((2, 4)),
            dma((5,)),
            dma((5,)),
        ],
        compiler_params=pltpu.CompilerParams(
            collective_id=0, has_side_effects=True, vmem_limit_bytes=60 * 1024 * 1024
        ),
        cost_estimate=pl.CostEstimate(
            flops=14 * 2 * rows * width * heads * HD,
            bytes_accessed=16 * width * heads * HD,
            transcendentals=2 * rows * heads * SEQ,
        ),
        name="fused",
    )(
        pattern.reshape(-1), input_norm_gain.reshape(1, width), q_gain.reshape(1, HD),
        k_gain.reshape(1, HD), tokens, grad_out, w_qkv, w_out,
    )[0]


def solution(mesh):
    fits = mesh.shape["dp"] == 16 and mesh.shape["tensor"] == 2
    return jax.shard_map(
        fused_body if fits else body,
        mesh=mesh,
        in_specs=(
            P("dp", "tensor"),
            P("dp", "tensor"),
            P(),
            P(),
            P(),
            P(None, "dp", "tensor"),
            P("tensor", "dp"),
            P("tensor", None, None),
        ),
        out_specs=P("dp", "tensor"),
        check_vma=False,
    )
```

```python
import functools
import math

import jax
import jax.numpy as jnp
from jax import lax
from jax.experimental import pallas as pl
from jax.experimental.pallas import tpu as pltpu
from jax.sharding import PartitionSpec as P

HD = 128
SEQ = 256
BLK = 64
EPS = 1e-06


def head_grads(query, key, value, upstream, q_gain, k_gain, listed, ksel):
    scale = 1.0 / math.sqrt(HD)
    blocks = SEQ // BLK
    column_block = lax.broadcasted_iota(jnp.int32, (BLK, SEQ), 1) // BLK

    def normalize(values):
        centred = values - jnp.mean(values, axis=-1, keepdims=True)
        inverse = lax.rsqrt(jnp.mean(centred * centred, axis=-1, keepdims=True) + EPS)
        return centred * inverse, inverse

    def pull_back(grad, hat, inverse, gain):
        d_hat = grad * gain
        return inverse * (
            d_hat
            - jnp.mean(d_hat, axis=-1, keepdims=True)
            - hat * jnp.mean(d_hat * hat, axis=-1, keepdims=True)
        )

    def dot(a, b, dims, precision=None):
        return lax.dot_general(
            a, b, (dims, ((), ())), precision=precision, preferred_element_type=jnp.float32
        )

    q_hat, q_inverse = normalize(query)
    k_hat, k_inverse = normalize(key)
    q_normed = q_hat * q_gain
    k_normed = k_hat * k_gain
    scores = dot(q_normed * scale, k_normed, ((1,), (1,)), lax.Precision.HIGHEST)
    rows = []
    for i in range(blocks):
        hit = column_block == listed(i, 0)
        for s in range(1, ksel):
            hit = hit | (column_block == listed(i, s))
        rows.append(jnp.where(hit, jnp.exp(scores[i * BLK : (i + 1) * BLK]), 0.0))
    weights = jnp.concatenate(rows, axis=0)
    probs = weights / jnp.sum(weights, axis=-1, keepdims=True)
    d_probs = dot(upstream, value, ((1,), (1,)))
    d_value = dot(probs.astype(jnp.bfloat16), upstream, ((0,), (0,)))
    d_scores = probs * (d_probs - jnp.sum(probs * d_probs, axis=-1, keepdims=True))
    d_scores = (d_scores * scale).astype(jnp.bfloat16)
    d_q = dot(d_scores, k_normed.astype(jnp.bfloat16), ((1,), (0,)))
    d_k = dot(d_scores, q_normed.astype(jnp.bfloat16), ((0,), (0,)))
    return (
        pull_back(d_q, q_hat, q_inverse, q_gain).astype(jnp.bfloat16),
        pull_back(d_k, k_hat, k_inverse, k_gain).astype(jnp.bfloat16),
        d_value.astype(jnp.bfloat16),
    )


def attention_kernel(ksel, pattern_ref, q_gain_ref, k_gain_ref, qkv_ref, up_ref, out_ref):
    head = pl.program_id(1)
    blocks = SEQ // BLK
    d_q, d_k, d_v = head_grads(
        qkv_ref[:, :HD].astype(jnp.float32),
        qkv_ref[:, HD : 2 * HD].astype(jnp.float32),
        qkv_ref[:, 2 * HD :],
        up_ref[...],
        q_gain_ref[...], k_gain_ref[...],
        lambda i, s: pattern_ref[(head * blocks + i) * ksel + s],
        ksel,
    )
    out_ref[:, :HD] = d_q
    out_ref[:, HD : 2 * HD] = d_k
    out_ref[:, 2 * HD :] = d_v


def attention_grads(qkv, upstream, q_gain, k_gain, pattern):
    rows, width = upstream.shape
    heads = width // HD
    images = rows // SEQ
    return pl.pallas_call(
        functools.partial(attention_kernel, pattern.shape[2]),
        grid=(images, heads),
        out_shape=jax.ShapeDtypeStruct((rows, 3 * width), jnp.bfloat16),
        in_specs=[
            pl.BlockSpec(memory_space=pltpu.SMEM),
            pl.BlockSpec((1, HD), lambda i, h: (0, 0)),
            pl.BlockSpec((1, HD), lambda i, h: (0, 0)),
            pl.BlockSpec((SEQ, 3 * HD), lambda i, h: (i, h)),
            pl.BlockSpec((SEQ, HD), lambda i, h: (i, h)),
        ],
        out_specs=pl.BlockSpec((SEQ, 3 * HD), lambda i, h: (i, h)),
        cost_estimate=pl.CostEstimate(
            flops=images * heads * 20 * SEQ * SEQ * HD,
            bytes_accessed=rows * width * 14,
            transcendentals=images * heads * SEQ * SEQ,
        ),
    )(pattern.reshape(-1), q_gain.reshape(1, HD), k_gain.reshape(1, HD), qkv, upstream)


def piece_kernel(sizes, qkv_ref, out_ref, *piece_refs):
    start = 0
    for size, piece_ref in zip(sizes, piece_refs):
        for head in range(size):
            cols = slice((start + head) * HD, (start + head + 1) * HD)
            for part in range(3):
                lo = (3 * head + part) * HD
                piece_ref[:, lo : lo + HD] = qkv_ref[part, :, cols]
        cols = slice(start * HD, (start + size) * HD)
        piece_ref[:, 3 * size * HD :] = out_ref[cols, :].T
        start += size


def weight_pieces(w_qkv, w_out, sizes):
    depth, width = w_qkv.shape[1:]
    step = HD if depth % HD == 0 else depth
    return pl.pallas_call(
        functools.partial(piece_kernel, sizes),
        grid=(depth // step,),
        out_shape=[
            jax.ShapeDtypeStruct((depth, 4 * size * HD), w_qkv.dtype) for size in sizes
        ],
        in_specs=[
            pl.BlockSpec((3, step, width), lambda i: (0, i, 0)),
            pl.BlockSpec((width, step), lambda i: (0, i)),
        ],
        out_specs=[pl.BlockSpec((step, 4 * size * HD), lambda i: (i, 0)) for size in sizes],
        cost_estimate=pl.CostEstimate(
            flops=0, bytes_accessed=16 * depth * width, transcendentals=0
        ),
    )(w_qkv, w_out)


def projection_kernel(steps, rows_ref, grads_ref, weight_ref, qkv_ref, up_ref, qkv_sum, up_sum):
    step = pl.program_id(0)
    span = qkv_ref.shape[1]

    @pl.when(step == 0)
    def _():
        qkv_sum[...] = jnp.zeros_like(qkv_sum)
        up_sum[...] = jnp.zeros_like(up_sum)

    qkv_sum[...] += jnp.dot(
        rows_ref[...], weight_ref[:, :span], preferred_element_type=jnp.float32
    )
    up_sum[...] += jnp.dot(
        grads_ref[...], weight_ref[:, span:], preferred_element_type=jnp.float32
    )

    @pl.when(step == steps - 1)
    def _():
        qkv_ref[...] = qkv_sum[...].astype(qkv_ref.dtype)
        up_ref[...] = up_sum[...].astype(up_ref.dtype)


def project(normed, grads, weight):
    rows, depth = normed.shape
    width = weight.shape[1] // 4
    block = 1024 if depth % 1024 == 0 else depth
    steps = depth // block
    return pl.pallas_call(
        functools.partial(projection_kernel, steps),
        grid=(steps,),
        out_shape=[
            jax.ShapeDtypeStruct((rows, 3 * width), jnp.bfloat16),
            jax.ShapeDtypeStruct((rows, width), jnp.bfloat16),
        ],
        in_specs=[
            pl.BlockSpec((rows, block), lambda k: (0, k)),
            pl.BlockSpec((rows, block), lambda k: (0, k)),
            pl.BlockSpec((block, 4 * width), lambda k: (k, 0)),
        ],
        out_specs=[
            pl.BlockSpec((rows, 3 * width), lambda k: (0, 0)),
            pl.BlockSpec((rows, width), lambda k: (0, 0)),
        ],
        scratch_shapes=[
            pltpu.VMEM((rows, 3 * width), jnp.float32),
            pltpu.VMEM((rows, width), jnp.float32),
        ],
        compiler_params=pltpu.CompilerParams(vmem_limit_bytes=32 * 1024 * 1024),
        cost_estimate=pl.CostEstimate(
            flops=8 * rows * depth * width,
            bytes_accessed=8 * depth * width + 4 * rows * depth,
            transcendentals=0,
        ),
    )(normed, grads, weight)


def head_chunks(heads):
    last = max(1, heads // 4)
    return [size for size in (heads - last, last) if size > 0]


def body(tokens, grad_out, input_norm_gain, q_gain, k_gain, w_qkv, w_out, pattern):
    row_count, width = tokens.shape
    parts = lax.axis_size("tensor")
    me = lax.axis_index("tensor")
    local_heads = w_qkv.shape[2] // HD

    sizes = head_chunks(local_heads)
    pieces = weight_pieces(w_qkv, w_out, sizes)
    gathered = [lax.all_gather(piece, "dp", axis=0, tiled=True) for piece in pieces]

    def exchange(value, shift):
        return lax.ppermute(
            value, "tensor", [(source, (source + shift) % parts) for source in range(parts)]
        )

    def whole_rows(own):
        full = jnp.zeros((row_count, width * parts), own.dtype)
        full = lax.dynamic_update_slice_in_dim(full, own, me * width, 1)
        for shift in range(1, parts):
            full = lax.dynamic_update_slice_in_dim(
                full, exchange(own, shift), lax.rem(me + parts - shift, parts) * width, 1
            )
        return full

    values = whole_rows(tokens).astype(jnp.float32)
    grads_full = whole_rows(grad_out)
    centre = jnp.mean(values, axis=-1, keepdims=True)
    centred = values - centre
    inverse = lax.rsqrt(jnp.mean(centred * centred, axis=-1, keepdims=True) + EPS)
    hat = centred * inverse
    normed = (hat * input_norm_gain).astype(jnp.bfloat16)
    normed, grads_full = lax.optimization_barrier((normed, grads_full))

    def own_columns(array, index, axis):
        return lax.dynamic_slice_in_dim(array, index * width, width, axis)

    targets = [lax.rem(me + shift, parts) for shift in range(parts)]
    totals = [None] * parts
    received = []
    start = 0
    for size, weight in zip(sizes, gathered):
        span = size * HD
        last = start + size == local_heads
        if last:
            qkv, upstream = project(normed, grads_full, weight)
        else:
            qkv = jnp.dot(
                normed, weight[:, : 3 * span], preferred_element_type=jnp.float32
            ).astype(jnp.bfloat16)
            upstream = jnp.dot(
                grads_full, weight[:, 3 * span :], preferred_element_type=jnp.float32
            ).astype(jnp.bfloat16)
        d_qkv = attention_grads(
            qkv, upstream, q_gain, k_gain, pattern[start : start + size]
        )
        for shift in [*range(1, parts), 0]:
            rows = own_columns(weight, targets[shift], 0)[:, : 3 * span]
            halves = 2 if last and shift else 1
            cut = width // halves
            sums_of, arrived = [], []
            for half in range(halves):
                part = slice(half * cut, (half + 1) * cut)
                term = lax.dot_general(
                    d_qkv,
                    rows[part],
                    (((1,), (1,)), ((), ())),
                    preferred_element_type=jnp.float32,
                )
                total = term if totals[shift] is None else totals[shift][:, part] + term
                if last and shift:
                    outgoing, total, d_qkv = lax.optimization_barrier(
                        (total.astype(jnp.bfloat16), total, d_qkv)
                    )
                    arrived.append(exchange(outgoing, shift))
                sums_of.append(total)
            totals[shift] = jnp.concatenate(sums_of, axis=1) if halves > 1 else sums_of[0]
            if arrived:
                received.append(jnp.concatenate(arrived, axis=1))
        start += size
        if not last:
            normed, grads_full, totals = lax.optimization_barrier((normed, grads_full, totals))

    sums = jnp.zeros((row_count, 2), jnp.float32)
    for shift in range(parts):
        gain = own_columns(input_norm_gain, targets[shift], 0)
        scaled = totals[shift] * gain
        sums = sums + jnp.stack(
            [
                jnp.sum(scaled, axis=-1),
                jnp.sum(scaled * own_columns(hat, targets[shift], 1), axis=-1),
            ],
            axis=1,
        )
    means = sums
    for shift in range(1, parts):
        means = means + exchange(sums, shift)
    means = means / (width * parts)
    d_normed = totals[0]
    for term in received:
        d_normed = d_normed + term.astype(jnp.float32)
    d_hat = d_normed * own_columns(input_norm_gain, me, 0)
    result = inverse * (d_hat - means[:, :1] - own_columns(hat, me, 1) * means[:, 1:])
    return result.astype(jnp.bfloat16)


CUTS = 4


def fused_kernel(
    heads, ksel, pattern_ref, gain_ref, q_gain_ref, k_gain_ref, tok_hbm, grad_hbm, wqkv, wout,
    out_ref, wq_all, wo_all,
    normed, grads, tok_own, total, slot_qkv, slot_out, qkv_sum, up_sum, d_qkv,
    mean_ref, inverse_ref, x_out, x_in, z_out, z_in, x_out2, x_in2, z_out2, z_in2, sums, sums_out, sums_in,
    local_sem, act_send, act_recv, z_send, z_recv, y_send, y_recv, c_send, c_recv, own_sem,
    load_sem, r_send, r_recv,
):
    depth = wqkv.shape[1]
    rows, half = tok_hbm.shape
    width = 2 * half
    quarter = half // 2
    me = lax.axis_index("dp")
    x = lax.axis_index("tensor")
    z = me // 4
    y = (me // 2) % 2
    c = me % 2
    p = z % 2
    inner = (z == 1) | (z == 2)
    window = 2 * CUTS
    units = heads * CUTS
    planes = {0: z, 1: z + 1 - 2 * p, 2: (z + 2) % 4, 3: 3 - z}

    def block_of(plane, row, core):
        return plane * 4 + row * 2 + core

    z_peer = {k: {"dp": block_of(planes[k], y, c), "tensor": x} for k in (1, 2, 3)}
    y_peer = {"dp": block_of(z, 1 - y, c), "tensor": x}
    c_peer = {"dp": block_of(z, y, 1 - c), "tensor": x}
    x_peer = {"dp": me, "tensor": 1 - x}
    far_peer = {"dp": block_of(planes[1], y, c), "tensor": 1 - x}
    peers = [z_peer[1], z_peer[2], z_peer[3], y_peer, c_peer, x_peer, far_peer]

    barrier = pltpu.get_barrier_semaphore()
    for peer in peers:
        pl.semaphore_signal(barrier, inc=1, device_id=peer, device_id_type=pl.DeviceIdType.MESH)
    pl.semaphore_wait(barrier, len(peers))

    def remote(src, dst, send, recv, peer):
        return pltpu.make_async_remote_copy(
            src_ref=src, dst_ref=dst, send_sem=send, recv_sem=recv,
            device_id=peer, device_id_type=pl.DeviceIdType.MESH,
        )

    own_rows = pl.ds(pl.multiple_of(p * rows, rows), rows)
    pair_rows = pl.ds(pl.multiple_of((1 - p) * rows, rows), rows)
    own_cols = pl.ds(pl.multiple_of(x * half, half), half)

    acts = ((tok_hbm, normed), (grad_hbm, grads))

    def act_local(i):
        return pltpu.make_async_copy(
            acts[i][0], acts[i][1].at[own_rows, own_cols], local_sem.at[i]
        )

    def act_z(i):
        return remote(
            acts[i][0], acts[i][1].at[own_rows, own_cols], act_send.at[i, 0], act_recv.at[i, 0], z_peer[1]
        )

    def act_x(i):
        return remote(
            acts[i][0], acts[i][1].at[own_rows, own_cols], act_send.at[i, 1], act_recv.at[i, 1], x_peer
        )

    def act_forward(i):
        part = acts[i][1].at[pair_rows, own_cols]
        return remote(part, part, act_send.at[i, 2], act_recv.at[i, 2], x_peer)

    cut = depth // CUTS
    cut_out = HD // CUTS

    def source(unit, group):
        head, part = unit // CUTS, unit % CUTS
        column = (group * heads + head) * HD
        rows_out = pl.ds(pl.multiple_of(column + part * cut_out, cut_out), cut_out)
        return (
            wqkv.at[:, pl.ds(pl.multiple_of(part * cut, cut), cut), pl.ds(pl.multiple_of(column, HD), HD)],
            wout.at[rows_out, :],
        )

    def place(unit, block):
        head, part = unit // CUTS, unit % CUTS
        at = pl.ds(pl.multiple_of(block * depth + part * cut, cut), cut)
        return (
            wq_all.at[head, :, at, :],
            wo_all.at[
                head,
                pl.ds(pl.multiple_of(part * cut_out, cut_out), cut_out),
                pl.ds(pl.multiple_of(block * depth, depth), depth),
            ],
        )

    def z_copies(unit, k):
        group = p if k == 2 else 1 - p
        return [
            remote(src, dst, z_send.at[unit, k - 1, i], z_recv.at[unit, k - 1, i], z_peer[k])
            for i, (src, dst) in enumerate(zip(source(unit, group), place(unit, me)))
        ]

    def y_copies(unit, k):
        part = place(unit, block_of(planes[k], y, c))
        return [
            remote(ref, ref, y_send.at[unit, k, i], y_recv.at[unit, k, i], y_peer)
            for i, ref in enumerate(part)
        ]

    def c_copies(unit, k, over):
        part = place(unit, block_of(planes[k], (1 - y) if over else y, c))
        head = unit // CUTS
        return [
            remote(ref, ref, c_send.at[head, i], c_recv.at[head, i], c_peer)
            for i, ref in enumerate(part)
        ]

    def head_source(head):
        cols = pl.ds(pl.multiple_of((p * heads + head) * HD, HD), HD)
        return wqkv.at[:, :, cols], wout.at[cols, :]

    def head_place(head, block):
        at = pl.ds(pl.multiple_of(block * depth, depth), depth)
        return wq_all.at[head, :, at, :], wo_all.at[head, :, at]

    def y_own(head):
        return [
            remote(s, d, y_send.at[head * CUTS, 0, i], y_recv.at[head * CUTS, 0, i], y_peer)
            for i, (s, d) in enumerate(zip(head_source(head), head_place(head, me)))
        ]

    def y_own_arrival(head):
        here = head_place(head, block_of(z, 1 - y, c))
        return [
            remote(d, d, y_send.at[head * CUTS, 0, i], y_recv.at[head * CUTS, 0, i], y_peer)
            for i, d in enumerate(here)
        ]

    def c_head(head, k, over):
        where = head_place(head, block_of(planes[k], (1 - y) if over else y, c))
        src = head_source(head) if k == 0 and not over else where
        return [
            remote(s, d, c_send.at[head, i], c_recv.at[head, i], c_peer)
            for i, (s, d) in enumerate(zip(src, where))
        ]

    def c_whole(head):
        whole = (
            wq_all.at[head, :, pl.ds(0, 8 * depth), :],
            wo_all.at[head, :, pl.ds(0, 8 * depth)],
        )
        return [
            remote(w, w, c_send.at[head, i], c_recv.at[head, i], c_peer) for i, w in enumerate(whole)
        ]

    def own_copies(head, back):
        part = pl.ds(pl.multiple_of(head * depth, depth), depth)
        cols = pl.ds(pl.multiple_of((p * heads + head) * HD, HD), HD)
        mine = pl.ds(pl.multiple_of(me * depth, depth), depth)
        legs = [
            (
                wqkv.at[i, :, cols],
                slot_qkv.at[part, pl.ds(i * HD, HD)],
                wq_all.at[head, i, mine, :],
            )
            for i in range(3)
        ]
        legs.append((wout.at[cols, :], slot_out.at[:HD, part], wo_all.at[head, :, mine]))
        return [
            pltpu.make_async_copy(*((mid, last) if back else (first, mid)), own_sem.at[head, i])
            for i, (first, mid, last) in enumerate(legs)
        ]

    def start(copies):
        for copy in copies:
            copy.start()

    def forward_own(head):
        start(y_own(head))
        start(c_head(head, 0, False))

    def forward(unit, k):
        for copy in z_copies(unit, k):
            copy.wait_recv()
        start(y_copies(unit, k))

        @pl.when(unit // CUTS == heads - 1)
        def _():
            start(c_copies(unit, k, False))

    def advance(unit, k):
        forward(unit, k)

        @pl.when(unit + window < units)
        def _():
            start(z_copies(unit + window, k))

    def stage_b(unit):
        head, part = unit // CUTS, unit % CUTS

        @pl.when(part == 0)
        def _():
            for copy in y_own_arrival(head):
                copy.wait_recv()
            start(c_head(head, 0, True))

        for k in (3, 1, 2):
            for copy in y_copies(unit, k):
                copy.wait_recv()

        @pl.when(head == heads - 1)
        def _():
            for k in (3, 1, 2):
                start(c_copies(unit, k, True))

        @pl.when((head < heads - 1) & (part == CUTS - 1))
        def _():
            for k in (3, 1, 2):
                start(c_head(head, k, False))
                start(c_head(head, k, True))

    def load_copies(head):
        pos = head % 2
        copies = [
            pltpu.make_async_copy(
                wq_all.at[head, i],
                slot_qkv.at[:, pl.ds(pl.multiple_of((pos * 3 + i) * HD, HD), HD)],
                load_sem.at[pos, i],
            )
            for i in range(3)
        ]
        copies.append(
            pltpu.make_async_copy(
                wo_all.at[head],
                slot_out.at[pl.ds(pl.multiple_of(pos * HD, HD), HD), :],
                load_sem.at[pos, 3],
            )
        )
        return copies

    def load(head):
        for copy in c_whole(head):
            copy.wait_recv()
        start(load_copies(head))

    def loaded(head):
        for copy in load_copies(head):
            copy.wait()

    q_gain = q_gain_ref[...]
    k_gain = k_gain_ref[...]
    blocks = SEQ // BLK

    def normalize_rows(first, count):
        step = 16

        def one(i, _):
            part = pl.ds(pl.multiple_of(first + i * step, step), step)
            values = normed[part, :].astype(jnp.float32)
            mean = jnp.mean(values, axis=-1, keepdims=True)
            centred = values - mean
            inverse = lax.rsqrt(jnp.mean(centred * centred, axis=-1, keepdims=True) + EPS)
            mean_ref[part, :] = mean
            inverse_ref[part, :] = inverse
            normed[part, :] = (centred * inverse * gain_ref[...]).astype(jnp.bfloat16)
            return 0

        lax.fori_loop(0, count // step, one, 0)

    def span_of(third, i):
        step = width // 6
        return pl.ds(pl.multiple_of((third * 2 + i) * step, step), step)

    def project(heads_of, third):
        cols = slice(heads_of[0] * 3 * HD, (heads_of[-1] + 1) * 3 * HD)

        @pl.when(third == 0)
        def _():
            qkv_sum[:, cols] = jnp.zeros_like(qkv_sum[:, cols])

        def one(i, _):
            part = span_of(third, i)
            qkv_sum[:, cols] += jnp.dot(
                normed[:, part], slot_qkv[part, cols], preferred_element_type=jnp.float32
            )
            return 0

        lax.fori_loop(0, 2, one, 0)

    def project_up(heads_of, third):
        cols = slice(heads_of[0] * HD, (heads_of[-1] + 1) * HD)

        @pl.when(third == 0)
        def _():
            up_sum[:, cols] = jnp.zeros_like(up_sum[:, cols])

        def one(i, _):
            part = span_of(third, i)
            up_sum[:, cols] += lax.dot_general(
                grads[:, part], slot_out[cols, part], (((1,), (1,)), ((), ())),
                preferred_element_type=jnp.float32,
            )
            return 0

        lax.fori_loop(0, 2, one, 0)

    def attend(pair, which):
        def one(image, _):
            part = pl.ds(pl.multiple_of(image * SEQ, SEQ), SEQ)
            cols = [pl.ds(pl.multiple_of((which * 3 + j) * HD, HD), HD) for j in range(3)]
            up_cols = pl.ds(pl.multiple_of(which * HD, HD), HD)
            results = head_grads(
                qkv_sum[part, cols[0]].astype(jnp.bfloat16).astype(jnp.float32),
                qkv_sum[part, cols[1]].astype(jnp.bfloat16).astype(jnp.float32),
                qkv_sum[part, cols[2]].astype(jnp.bfloat16),
                up_sum[part, up_cols].astype(jnp.bfloat16),
                q_gain, k_gain,
                lambda i, s: pattern_ref[((p * heads + 2 * pair + which) * blocks + i) * ksel + s],
                ksel,
            )
            for j in range(3):
                d_qkv[part, cols[j]] = results[j]
            return 0

        lax.fori_loop(0, 2 * rows // SEQ, one, 0)

    def add_cols(which, part_of):
        step = 512
        base = which * half + part_of * quarter

        def one(i, _):
            part = pl.ds(pl.multiple_of(base + i * step, step), step)
            total[:, part] += lax.dot_general(
                d_qkv[...], slot_qkv[part, :], (((1,), (1,)), ((), ())),
                preferred_element_type=jnp.float32,
            )
            return 0

        lax.fori_loop(0, quarter // step, one, 0)

    act_z(0).start()
    act_x(0).start()

    def each_head(act, low=0, high=heads):
        def one(head, _):
            act(head)
            return 0

        lax.fori_loop(low, high, one, 0)

    @pl.when(inner)
    def _():
        each_head(lambda unit: start(z_copies(unit, 3)), 0, units)

    each_head(forward_own)
    each_head(lambda head: start(own_copies(head, False)))
    for i in range(2):
        act_local(i).start()
    tok_copy = pltpu.make_async_copy(tok_hbm, tok_own, local_sem.at[2])
    tok_copy.start()
    total[...] = jnp.zeros_like(total)

    def turn_own(head):
        for copy in own_copies(head, False):
            copy.wait()
        start(own_copies(head, True))

    each_head(turn_own)

    @pl.when(inner)
    def _():
        each_head(lambda unit: forward(unit, 3), 0, units // 2)

    act_z(0).wait_send()
    act_z(1).start()
    act_z(0).wait_recv()
    act_forward(0).start()

    @pl.when(inner)
    def _():
        each_head(lambda unit: forward(unit, 3), units // 2, units)

    act_z(1).wait_recv()
    act_x(1).start()
    act_forward(1).start()
    act_z(1).wait_send()

    def first_units(unit):
        for k in (1, 2):
            start(z_copies(unit, k))

        @pl.when(jnp.logical_not(inner))
        def _():
            start(z_copies(unit, 3))

    each_head(first_units, 0, window)

    def wait_own(head):
        for copy in own_copies(head, True):
            copy.wait()

    each_head(wait_own)

    def third_step(t):
        unit, k = t // 3, t % 3

        @pl.when(k == 0)
        def _():
            advance(unit, 1)

        @pl.when(k == 1)
        def _():
            advance(unit, 2)

        @pl.when((k == 2) & jnp.logical_not(inner))
        def _():
            advance(unit, 3)

        @pl.when((k == 2) & (unit > 0))
        def _():
            stage_b(unit - 1)

        def arrived(i):
            act_local(i).wait()
            act_x(i).wait()
            act_forward(i).wait()

        @pl.when(t == 2)
        def _():
            arrived(0)

        @pl.when((t >= 3) & (t < 7))
        def _():
            normalize_rows((t - 3) * (rows // 2), rows // 2)

        @pl.when(t == 18)
        def _():
            load(0)

        @pl.when(t == 29)
        def _():
            load(1)

        @pl.when(t == 31)
        def _():
            loaded(0)
            loaded(1)

        @pl.when(t == 55)
        def _():
            loaded(2)
            loaded(3)

        @pl.when(((t >= 31) & (t < 34)) | ((t >= 55) & (t < 58)))
        def _():
            project((0, 1), (t - 31) % 24)

        @pl.when(t == 36)
        def _():
            arrived(1)

        @pl.when((t == 36) | (t == 58))
        def _():
            each_head(lambda third: project_up((0, 1), third), 0, 3)

        @pl.when((t == 37) | (t == 38) | (t == 59) | (t == 60) | (t == 71))
        def _():
            attend((t - 37) // 16, (t + 1) % 2)

        @pl.when((t == 39) | (t == 40) | (t == 61) | (t == 62))
        def _():
            add_cols((t + 1) % 2, 0)
            add_cols((t + 1) % 2, 1)

        @pl.when(t == 41)
        def _():
            load(2)

        @pl.when(t == 53)
        def _():
            load(3)

        @pl.when(t == 65)
        def _():
            load(4)

        @pl.when(t == 67)
        def _():
            loaded(4)

        @pl.when((t >= 67) & (t < 70))
        def _():
            project((0,), t - 67)
            project_up((0,), t - 67)

    each_head(third_step, 0, 3 * units)
    tok_copy.wait()
    stage_b(units - 1)
    load(5)
    loaded(5)
    for third in range(3):
        project((1,), third)
        project_up((1,), third)
    attend(2, 1)

    def block_cols(which, part):
        return pl.ds(pl.multiple_of(which * half + part * quarter, quarter), quarter)

    def reduce_leg(i, src, dst, peer):
        return remote(src, dst, r_send.at[i], r_recv.at[i], peer)

    x_legs = [reduce_leg(i, x_out.at[r], x_in.at[r], x_peer) for i, r in enumerate((pair_rows, own_rows))]
    z_legs = [
        reduce_leg(2 + i, z_out.at[w], z_in.at[w], z_peer[1]) for i, w in enumerate((1 - x, x))
    ]
    z_last = reduce_leg(4, z_out2, z_in2, z_peer[1])
    x_last = reduce_leg(5, x_out2, x_in2, x_peer)
    for leg, r in zip(x_legs, (pair_rows, own_rows)):
        if leg is x_legs[0]:
            add_cols(1 - x, 0)
        x_out[r, :] = total[r, block_cols(1 - x, 0)].astype(jnp.bfloat16)
        leg.start()
    for leg, w in zip(z_legs, (1 - x, x)):
        add_cols(w, 1)
        z_out[w] = total[pair_rows, block_cols(w, 1)].astype(jnp.bfloat16)
        leg.start()
    add_cols(x, 0)

    step = 16
    lane = lax.broadcasted_iota(jnp.int32, (step, 128), 1)

    def sum_rows(i):
        part = pl.ds(pl.multiple_of(i * step, step), step)
        share = total[part, :]
        first = jnp.sum(share * gain_ref[...], axis=-1, keepdims=True)
        second = jnp.sum(share * normed[part, :].astype(jnp.float32), axis=-1, keepdims=True)
        sums[part, :] = jnp.where(lane == 0, first, jnp.where(lane == 1, second, 0.0))

    each_head(sum_rows, 0, 2 * rows // step)
    sums_out[0] = sums[own_rows, :].T[:8]
    sums_out[1] = sums[pair_rows, :].T[:8]
    sum_legs = [
        reduce_leg(6, sums_out.at[0], sums_in.at[0], x_peer),
        reduce_leg(7, sums_out.at[1], sums_in.at[1], z_peer[1]),
        reduce_leg(8, sums_out.at[1], sums_in.at[2], far_peer),
    ]
    start(sum_legs)

    x_legs[0].wait_recv()
    z_out2[...] = (
        total[pair_rows, block_cols(x, 0)] + x_in[pair_rows, :].astype(jnp.float32)
    ).astype(jnp.bfloat16)
    z_last.start()
    z_legs[0].wait_recv()
    x_out2[...] = (
        total[own_rows, block_cols(1 - x, 1)] + z_in[1 - x].astype(jnp.float32)
    ).astype(jnp.bfloat16)
    x_last.start()
    for leg in sum_legs:
        leg.wait_recv()
    means = (sums_out[0] + sums_in[0] + sums_in[1] + sums_in[2]) / width
    sums[:rows, :] = jnp.concatenate([means, jnp.zeros((120, rows), jnp.float32)], axis=0).T
    x_legs[1].wait_recv()
    total[own_rows, block_cols(x, 0)] += x_in[own_rows, :].astype(jnp.float32)
    z_legs[1].wait_recv()
    total[own_rows, block_cols(x, 1)] += z_in[x].astype(jnp.float32)

    def finish(part_of, arrived):
        cols = block_cols(x, part_of)
        here = slice(part_of * quarter, (part_of + 1) * quarter)

        def one(i):
            part = pl.ds(pl.multiple_of(i * step, step), step)
            shifted = pl.ds(pl.multiple_of(p * rows + i * step, step), step)
            inverse = inverse_ref[shifted, :]
            hat = (tok_own[part, here].astype(jnp.float32) - mean_ref[shifted, :]) * inverse
            d_hat = (total[shifted, cols] + arrived[part, :].astype(jnp.float32)) * gain_ref[:, cols]
            row_means = sums[part, :]
            out_ref[part, here] = (
                inverse * (d_hat - row_means[:, :1] - hat * row_means[:, 1:2])
            ).astype(jnp.bfloat16)

        each_head(one, 0, rows // step)

    z_last.wait_recv()
    finish(0, z_in2)
    x_last.wait_recv()
    finish(1, x_in2)

    for copy in (*x_legs, *z_legs, z_last, x_last, *sum_legs):
        copy.wait_send()

    def drain(unit):
        for k in (1, 2, 3):
            for copy in (*z_copies(unit, k), *y_copies(unit, k)):
                copy.wait_send()

    each_head(drain, 0, units)

    def drain_core(head):
        for copy in y_own(head):
            copy.wait_send()
        for copy in c_whole(head):
            copy.wait_send()

    each_head(drain_core)


def fused_body(tokens, grad_out, input_norm_gain, q_gain, k_gain, w_qkv, w_out, pattern):
    rows, half = tokens.shape
    depth = w_qkv.shape[1]
    width = 2 * half
    heads = w_qkv.shape[2] // HD // 2
    quarter = half // 2
    dma = pltpu.SemaphoreType.DMA
    bf16, f32 = jnp.bfloat16, jnp.float32
    vmem = pl.BlockSpec(memory_space=pltpu.VMEM)
    hbm = pl.BlockSpec(memory_space=pl.ANY)
    return pl.pallas_call(
        functools.partial(fused_kernel, heads, pattern.shape[2]),
        out_shape=[
            jax.ShapeDtypeStruct((rows, half), bf16),
            jax.ShapeDtypeStruct((heads, 3, width, HD), bf16),
            jax.ShapeDtypeStruct((heads, HD, width), bf16),
        ],
        in_specs=[pl.BlockSpec(memory_space=pltpu.SMEM), vmem, vmem, vmem, hbm, hbm, hbm, hbm],
        out_specs=[vmem, hbm, hbm],
        scratch_shapes=[
            pltpu.VMEM((2 * rows, width), bf16),
            pltpu.VMEM((2 * rows, width), bf16),
            pltpu.VMEM((rows, half), bf16),
            pltpu.VMEM((2 * rows, width), f32),
            pltpu.VMEM((width, 6 * HD), bf16),
            pltpu.VMEM((2 * HD, width), bf16),
            pltpu.VMEM((2 * rows, 6 * HD), f32),
            pltpu.VMEM((2 * rows, 2 * HD), f32),
            pltpu.VMEM((2 * rows, 6 * HD), bf16),
            pltpu.VMEM((2 * rows, 1), f32),
            pltpu.VMEM((2 * rows, 1), f32),
            pltpu.VMEM((2 * rows, quarter), bf16),
            pltpu.VMEM((2 * rows, quarter), bf16),
            pltpu.VMEM((2, rows, quarter), bf16),
            pltpu.VMEM((2, rows, quarter), bf16),
            pltpu.VMEM((rows, quarter), bf16),
            pltpu.VMEM((rows, quarter), bf16),
            pltpu.VMEM((rows, quarter), bf16),
            pltpu.VMEM((rows, quarter), bf16),
            pltpu.VMEM((2 * rows, 128), f32),
            pltpu.VMEM((2, 8, rows), f32),
            pltpu.VMEM((3, 8, rows), f32),
            dma((3,)),
            dma((2, 3)),
            dma((2, 3)),
            dma((heads * CUTS, 3, 2)),
            dma((heads * CUTS, 3, 2)),
            dma((heads * CUTS, 4, 2)),
            dma((heads * CUTS, 4, 2)),
            dma((heads, 2)),
            dma((heads, 2)),
            dma((heads, 4)),
            dma((2, 4)),
            dma((9,)),
            dma((9,)),
        ],
        compiler_params=pltpu.CompilerParams(
            collective_id=0, has_side_effects=True, vmem_limit_bytes=60 * 1024 * 1024
        ),
        cost_estimate=pl.CostEstimate(
            flops=14 * 2 * rows * width * heads * HD,
            bytes_accessed=16 * width * heads * HD,
            transcendentals=2 * rows * heads * SEQ,
        ),
        name="fused",
    )(
        pattern.reshape(-1), input_norm_gain.reshape(1, width), q_gain.reshape(1, HD),
        k_gain.reshape(1, HD), tokens, grad_out, w_qkv, w_out,
    )[0]


def choose(*args):
    fits = lax.axis_size("dp") == 16 and lax.axis_size("tensor") == 2
    fits = fits and args[0].shape[0] == SEQ and args[5].shape[2] == 12 * HD
    return (fused_body if fits else body)(*args)


def solution(mesh):
    return jax.shard_map(
        choose,
        mesh=mesh,
        in_specs=(
            P("dp", "tensor"),
            P("dp", "tensor"),
            P(),
            P(),
            P(),
            P(None, "dp", "tensor"),
            P("tensor", "dp"),
            P("tensor", None, None),
        ),
        out_specs=P("dp", "tensor"),
        check_vma=False,
    )
```

```python
import functools
import math

import jax
import jax.numpy as jnp
from jax import lax
from jax.experimental import pallas as pl
from jax.experimental.pallas import tpu as pltpu
from jax.sharding import PartitionSpec as P

HD = 128
SEQ = 256
BLK = 64
EPS = 1e-06


def head_grads(query, key, value, upstream, q_gain, k_gain, listed, ksel):
    scale = 1.0 / math.sqrt(HD)
    blocks = SEQ // BLK
    column_block = lax.broadcasted_iota(jnp.int32, (BLK, SEQ), 1) // BLK

    def normalize(values):
        centred = values - jnp.mean(values, axis=-1, keepdims=True)
        inverse = lax.rsqrt(jnp.mean(centred * centred, axis=-1, keepdims=True) + EPS)
        return centred * inverse, inverse

    def pull_back(grad, hat, inverse, gain):
        d_hat = grad * gain
        return inverse * (
            d_hat
            - jnp.mean(d_hat, axis=-1, keepdims=True)
            - hat * jnp.mean(d_hat * hat, axis=-1, keepdims=True)
        )

    def dot(a, b, dims, precision=None):
        return lax.dot_general(
            a, b, (dims, ((), ())), precision=precision, preferred_element_type=jnp.float32
        )

    q_hat, q_inverse = normalize(query)
    k_hat, k_inverse = normalize(key)
    q_normed = q_hat * q_gain
    k_normed = k_hat * k_gain
    scores = dot(q_normed * scale, k_normed, ((1,), (1,)), lax.Precision.HIGHEST)
    rows = []
    for i in range(blocks):
        hit = column_block == listed(i, 0)
        for s in range(1, ksel):
            hit = hit | (column_block == listed(i, s))
        rows.append(jnp.where(hit, jnp.exp(scores[i * BLK : (i + 1) * BLK]), 0.0))
    weights = jnp.concatenate(rows, axis=0)
    probs = weights / jnp.sum(weights, axis=-1, keepdims=True)
    d_probs = dot(upstream, value, ((1,), (1,)))
    d_value = dot(probs.astype(jnp.bfloat16), upstream, ((0,), (0,)))
    d_scores = probs * (d_probs - jnp.sum(probs * d_probs, axis=-1, keepdims=True))
    d_scores = (d_scores * scale).astype(jnp.bfloat16)
    d_q = dot(d_scores, k_normed.astype(jnp.bfloat16), ((1,), (0,)))
    d_k = dot(d_scores, q_normed.astype(jnp.bfloat16), ((0,), (0,)))
    return (
        pull_back(d_q, q_hat, q_inverse, q_gain).astype(jnp.bfloat16),
        pull_back(d_k, k_hat, k_inverse, k_gain).astype(jnp.bfloat16),
        d_value.astype(jnp.bfloat16),
    )


def attention_kernel(ksel, pattern_ref, q_gain_ref, k_gain_ref, qkv_ref, up_ref, out_ref):
    head = pl.program_id(1)
    blocks = SEQ // BLK
    d_q, d_k, d_v = head_grads(
        qkv_ref[:, :HD].astype(jnp.float32),
        qkv_ref[:, HD : 2 * HD].astype(jnp.float32),
        qkv_ref[:, 2 * HD :],
        up_ref[...],
        q_gain_ref[...], k_gain_ref[...],
        lambda i, s: pattern_ref[(head * blocks + i) * ksel + s],
        ksel,
    )
    out_ref[:, :HD] = d_q
    out_ref[:, HD : 2 * HD] = d_k
    out_ref[:, 2 * HD :] = d_v


def attention_grads(qkv, upstream, q_gain, k_gain, pattern):
    rows, width = upstream.shape
    heads = width // HD
    images = rows // SEQ
    return pl.pallas_call(
        functools.partial(attention_kernel, pattern.shape[2]),
        grid=(images, heads),
        out_shape=jax.ShapeDtypeStruct((rows, 3 * width), jnp.bfloat16),
        in_specs=[
            pl.BlockSpec(memory_space=pltpu.SMEM),
            pl.BlockSpec((1, HD), lambda i, h: (0, 0)),
            pl.BlockSpec((1, HD), lambda i, h: (0, 0)),
            pl.BlockSpec((SEQ, 3 * HD), lambda i, h: (i, h)),
            pl.BlockSpec((SEQ, HD), lambda i, h: (i, h)),
        ],
        out_specs=pl.BlockSpec((SEQ, 3 * HD), lambda i, h: (i, h)),
        cost_estimate=pl.CostEstimate(
            flops=images * heads * 20 * SEQ * SEQ * HD,
            bytes_accessed=rows * width * 14,
            transcendentals=images * heads * SEQ * SEQ,
        ),
    )(pattern.reshape(-1), q_gain.reshape(1, HD), k_gain.reshape(1, HD), qkv, upstream)


def piece_kernel(sizes, qkv_ref, out_ref, *piece_refs):
    start = 0
    for size, piece_ref in zip(sizes, piece_refs):
        for head in range(size):
            cols = slice((start + head) * HD, (start + head + 1) * HD)
            for part in range(3):
                lo = (3 * head + part) * HD
                piece_ref[:, lo : lo + HD] = qkv_ref[part, :, cols]
        cols = slice(start * HD, (start + size) * HD)
        piece_ref[:, 3 * size * HD :] = out_ref[cols, :].T
        start += size


def weight_pieces(w_qkv, w_out, sizes):
    depth, width = w_qkv.shape[1:]
    step = HD if depth % HD == 0 else depth
    return pl.pallas_call(
        functools.partial(piece_kernel, sizes),
        grid=(depth // step,),
        out_shape=[
            jax.ShapeDtypeStruct((depth, 4 * size * HD), w_qkv.dtype) for size in sizes
        ],
        in_specs=[
            pl.BlockSpec((3, step, width), lambda i: (0, i, 0)),
            pl.BlockSpec((width, step), lambda i: (0, i)),
        ],
        out_specs=[pl.BlockSpec((step, 4 * size * HD), lambda i: (i, 0)) for size in sizes],
        cost_estimate=pl.CostEstimate(
            flops=0, bytes_accessed=16 * depth * width, transcendentals=0
        ),
    )(w_qkv, w_out)


def projection_kernel(steps, rows_ref, grads_ref, weight_ref, qkv_ref, up_ref, qkv_sum, up_sum):
    step = pl.program_id(0)
    span = qkv_ref.shape[1]

    @pl.when(step == 0)
    def _():
        qkv_sum[...] = jnp.zeros_like(qkv_sum)
        up_sum[...] = jnp.zeros_like(up_sum)

    qkv_sum[...] += jnp.dot(
        rows_ref[...], weight_ref[:, :span], preferred_element_type=jnp.float32
    )
    up_sum[...] += jnp.dot(
        grads_ref[...], weight_ref[:, span:], preferred_element_type=jnp.float32
    )

    @pl.when(step == steps - 1)
    def _():
        qkv_ref[...] = qkv_sum[...].astype(qkv_ref.dtype)
        up_ref[...] = up_sum[...].astype(up_ref.dtype)


def project(normed, grads, weight):
    rows, depth = normed.shape
    width = weight.shape[1] // 4
    block = 1024 if depth % 1024 == 0 else depth
    steps = depth // block
    return pl.pallas_call(
        functools.partial(projection_kernel, steps),
        grid=(steps,),
        out_shape=[
            jax.ShapeDtypeStruct((rows, 3 * width), jnp.bfloat16),
            jax.ShapeDtypeStruct((rows, width), jnp.bfloat16),
        ],
        in_specs=[
            pl.BlockSpec((rows, block), lambda k: (0, k)),
            pl.BlockSpec((rows, block), lambda k: (0, k)),
            pl.BlockSpec((block, 4 * width), lambda k: (k, 0)),
        ],
        out_specs=[
            pl.BlockSpec((rows, 3 * width), lambda k: (0, 0)),
            pl.BlockSpec((rows, width), lambda k: (0, 0)),
        ],
        scratch_shapes=[
            pltpu.VMEM((rows, 3 * width), jnp.float32),
            pltpu.VMEM((rows, width), jnp.float32),
        ],
        compiler_params=pltpu.CompilerParams(vmem_limit_bytes=32 * 1024 * 1024),
        cost_estimate=pl.CostEstimate(
            flops=8 * rows * depth * width,
            bytes_accessed=8 * depth * width + 4 * rows * depth,
            transcendentals=0,
        ),
    )(normed, grads, weight)


def head_chunks(heads):
    last = max(1, heads // 4)
    return [size for size in (heads - last, last) if size > 0]


def body(tokens, grad_out, input_norm_gain, q_gain, k_gain, w_qkv, w_out, pattern):
    row_count, width = tokens.shape
    parts = lax.axis_size("tensor")
    me = lax.axis_index("tensor")
    local_heads = w_qkv.shape[2] // HD

    sizes = head_chunks(local_heads)
    pieces = weight_pieces(w_qkv, w_out, sizes)
    gathered = [lax.all_gather(piece, "dp", axis=0, tiled=True) for piece in pieces]

    def exchange(value, shift):
        return lax.ppermute(
            value, "tensor", [(source, (source + shift) % parts) for source in range(parts)]
        )

    def whole_rows(own):
        full = jnp.zeros((row_count, width * parts), own.dtype)
        full = lax.dynamic_update_slice_in_dim(full, own, me * width, 1)
        for shift in range(1, parts):
            full = lax.dynamic_update_slice_in_dim(
                full, exchange(own, shift), lax.rem(me + parts - shift, parts) * width, 1
            )
        return full

    values = whole_rows(tokens).astype(jnp.float32)
    grads_full = whole_rows(grad_out)
    centre = jnp.mean(values, axis=-1, keepdims=True)
    centred = values - centre
    inverse = lax.rsqrt(jnp.mean(centred * centred, axis=-1, keepdims=True) + EPS)
    hat = centred * inverse
    normed = (hat * input_norm_gain).astype(jnp.bfloat16)
    normed, grads_full = lax.optimization_barrier((normed, grads_full))

    def own_columns(array, index, axis):
        return lax.dynamic_slice_in_dim(array, index * width, width, axis)

    targets = [lax.rem(me + shift, parts) for shift in range(parts)]
    totals = [None] * parts
    received = []
    start = 0
    for size, weight in zip(sizes, gathered):
        span = size * HD
        last = start + size == local_heads
        if last:
            qkv, upstream = project(normed, grads_full, weight)
        else:
            qkv = jnp.dot(
                normed, weight[:, : 3 * span], preferred_element_type=jnp.float32
            ).astype(jnp.bfloat16)
            upstream = jnp.dot(
                grads_full, weight[:, 3 * span :], preferred_element_type=jnp.float32
            ).astype(jnp.bfloat16)
        d_qkv = attention_grads(
            qkv, upstream, q_gain, k_gain, pattern[start : start + size]
        )
        for shift in [*range(1, parts), 0]:
            rows = own_columns(weight, targets[shift], 0)[:, : 3 * span]
            halves = 2 if last and shift else 1
            cut = width // halves
            sums_of, arrived = [], []
            for half in range(halves):
                part = slice(half * cut, (half + 1) * cut)
                term = lax.dot_general(
                    d_qkv,
                    rows[part],
                    (((1,), (1,)), ((), ())),
                    preferred_element_type=jnp.float32,
                )
                total = term if totals[shift] is None else totals[shift][:, part] + term
                if last and shift:
                    outgoing, total, d_qkv = lax.optimization_barrier(
                        (total.astype(jnp.bfloat16), total, d_qkv)
                    )
                    arrived.append(exchange(outgoing, shift))
                sums_of.append(total)
            totals[shift] = jnp.concatenate(sums_of, axis=1) if halves > 1 else sums_of[0]
            if arrived:
                received.append(jnp.concatenate(arrived, axis=1))
        start += size
        if not last:
            normed, grads_full, totals = lax.optimization_barrier((normed, grads_full, totals))

    sums = jnp.zeros((row_count, 2), jnp.float32)
    for shift in range(parts):
        gain = own_columns(input_norm_gain, targets[shift], 0)
        scaled = totals[shift] * gain
        sums = sums + jnp.stack(
            [
                jnp.sum(scaled, axis=-1),
                jnp.sum(scaled * own_columns(hat, targets[shift], 1), axis=-1),
            ],
            axis=1,
        )
    means = sums
    for shift in range(1, parts):
        means = means + exchange(sums, shift)
    means = means / (width * parts)
    d_normed = totals[0]
    for term in received:
        d_normed = d_normed + term.astype(jnp.float32)
    d_hat = d_normed * own_columns(input_norm_gain, me, 0)
    result = inverse * (d_hat - means[:, :1] - own_columns(hat, me, 1) * means[:, 1:])
    return result.astype(jnp.bfloat16)


CUTS = 4


def fused_kernel(
    heads, ksel, pattern_ref, gain_ref, q_gain_ref, k_gain_ref, tok_hbm, grad_hbm, wqkv, wout,
    out_ref, wq_all, wo_all,
    normed, grads, tok_own, total, slot_qkv, slot_out, qkv_sum, up_sum, d_qkv,
    mean_ref, inverse_ref, x_out, x_in, z_out, z_in, x_out2, x_in2, z_out2, z_in2, sums, sums_out, sums_in,
    local_sem, act_send, act_recv, z_send, z_recv, y_send, y_recv, c_send, c_recv, own_sem,
    load_sem, r_send, r_recv,
):
    depth = wqkv.shape[1]
    rows, half = tok_hbm.shape
    width = 2 * half
    quarter = half // 2
    me = lax.axis_index("dp")
    x = lax.axis_index("tensor")
    z = me // 4
    y = (me // 2) % 2
    c = me % 2
    p = z % 2
    inner = (z == 1) | (z == 2)
    window = 2 * CUTS
    units = heads * CUTS
    planes = {0: z, 1: z + 1 - 2 * p, 2: (z + 2) % 4, 3: 3 - z}

    def block_of(plane, row, core):
        return plane * 4 + row * 2 + core

    z_peer = {k: {"dp": block_of(planes[k], y, c), "tensor": x} for k in (1, 2, 3)}
    y_peer = {"dp": block_of(z, 1 - y, c), "tensor": x}
    c_peer = {"dp": block_of(z, y, 1 - c), "tensor": x}
    x_peer = {"dp": me, "tensor": 1 - x}
    far_peer = {"dp": block_of(planes[1], y, c), "tensor": 1 - x}
    peers = [z_peer[1], z_peer[2], z_peer[3], y_peer, c_peer, x_peer, far_peer]

    barrier = pltpu.get_barrier_semaphore()
    for peer in peers:
        pl.semaphore_signal(barrier, inc=1, device_id=peer, device_id_type=pl.DeviceIdType.MESH)
    pl.semaphore_wait(barrier, len(peers))

    def remote(src, dst, send, recv, peer):
        return pltpu.make_async_remote_copy(
            src_ref=src, dst_ref=dst, send_sem=send, recv_sem=recv,
            device_id=peer, device_id_type=pl.DeviceIdType.MESH,
        )

    own_rows = pl.ds(pl.multiple_of(p * rows, rows), rows)
    pair_rows = pl.ds(pl.multiple_of((1 - p) * rows, rows), rows)
    own_cols = pl.ds(pl.multiple_of(x * half, half), half)

    acts = ((tok_hbm, normed), (grad_hbm, grads))

    def act_local(i):
        return pltpu.make_async_copy(
            acts[i][0], acts[i][1].at[own_rows, own_cols], local_sem.at[i]
        )

    def act_z(i):
        return remote(
            acts[i][0], acts[i][1].at[own_rows, own_cols], act_send.at[i, 0], act_recv.at[i, 0], z_peer[1]
        )

    def act_x(i):
        return remote(
            acts[i][0], acts[i][1].at[own_rows, own_cols], act_send.at[i, 1], act_recv.at[i, 1], x_peer
        )

    def act_forward(i):
        part = acts[i][1].at[pair_rows, own_cols]
        return remote(part, part, act_send.at[i, 2], act_recv.at[i, 2], x_peer)

    cut = depth // CUTS
    cut_out = HD // CUTS

    def source(unit, group):
        head, part = unit // CUTS, unit % CUTS
        column = (group * heads + head) * HD
        rows_out = pl.ds(pl.multiple_of(column + part * cut_out, cut_out), cut_out)
        return (
            wqkv.at[:, pl.ds(pl.multiple_of(part * cut, cut), cut), pl.ds(pl.multiple_of(column, HD), HD)],
            wout.at[rows_out, :],
        )

    def place(unit, block):
        head, part = unit // CUTS, unit % CUTS
        at = pl.ds(pl.multiple_of(block * depth + part * cut, cut), cut)
        return (
            wq_all.at[head, :, at, :],
            wo_all.at[
                head,
                pl.ds(pl.multiple_of(part * cut_out, cut_out), cut_out),
                pl.ds(pl.multiple_of(block * depth, depth), depth),
            ],
        )

    def z_copies(unit, k):
        group = p if k == 2 else 1 - p
        return [
            remote(src, dst, z_send.at[unit, k - 1, i], z_recv.at[unit, k - 1, i], z_peer[k])
            for i, (src, dst) in enumerate(zip(source(unit, group), place(unit, me)))
        ]

    def y_copies(unit, k):
        part = place(unit, block_of(planes[k], y, c))
        return [
            remote(ref, ref, y_send.at[unit, k, i], y_recv.at[unit, k, i], y_peer)
            for i, ref in enumerate(part)
        ]

    def c_copies(unit, k, over):
        part = place(unit, block_of(planes[k], (1 - y) if over else y, c))
        head = unit // CUTS
        return [
            remote(ref, ref, c_send.at[head, i], c_recv.at[head, i], c_peer)
            for i, ref in enumerate(part)
        ]

    def head_source(head):
        cols = pl.ds(pl.multiple_of((p * heads + head) * HD, HD), HD)
        return wqkv.at[:, :, cols], wout.at[cols, :]

    def head_place(head, block):
        at = pl.ds(pl.multiple_of(block * depth, depth), depth)
        return wq_all.at[head, :, at, :], wo_all.at[head, :, at]

    def y_own(head):
        return [
            remote(s, d, y_send.at[head * CUTS, 0, i], y_recv.at[head * CUTS, 0, i], y_peer)
            for i, (s, d) in enumerate(zip(head_source(head), head_place(head, me)))
        ]

    def y_own_arrival(head):
        here = head_place(head, block_of(z, 1 - y, c))
        return [
            remote(d, d, y_send.at[head * CUTS, 0, i], y_recv.at[head * CUTS, 0, i], y_peer)
            for i, d in enumerate(here)
        ]

    def c_head(head, k, over):
        where = head_place(head, block_of(planes[k], (1 - y) if over else y, c))
        src = head_source(head) if k == 0 and not over else where
        return [
            remote(s, d, c_send.at[head, i], c_recv.at[head, i], c_peer)
            for i, (s, d) in enumerate(zip(src, where))
        ]

    def c_whole(head):
        whole = (
            wq_all.at[head, :, pl.ds(0, 8 * depth), :],
            wo_all.at[head, :, pl.ds(0, 8 * depth)],
        )
        return [
            remote(w, w, c_send.at[head, i], c_recv.at[head, i], c_peer) for i, w in enumerate(whole)
        ]

    def own_copies(head, back):
        part = pl.ds(pl.multiple_of(head * depth, depth), depth)
        cols = pl.ds(pl.multiple_of((p * heads + head) * HD, HD), HD)
        mine = pl.ds(pl.multiple_of(me * depth, depth), depth)
        legs = [
            (
                wqkv.at[i, :, cols],
                slot_qkv.at[part, pl.ds(i * HD, HD)],
                wq_all.at[head, i, mine, :],
            )
            for i in range(3)
        ]
        legs.append((wout.at[cols, :], slot_out.at[:HD, part], wo_all.at[head, :, mine]))
        return [
            pltpu.make_async_copy(*((mid, last) if back else (first, mid)), own_sem.at[head, i])
            for i, (first, mid, last) in enumerate(legs)
        ]

    def start(copies):
        for copy in copies:
            copy.start()

    def forward_own(head):
        start(y_own(head))
        start(c_head(head, 0, False))

    def forward(unit, k):
        for copy in z_copies(unit, k):
            copy.wait_recv()
        start(y_copies(unit, k))

        @pl.when(unit // CUTS == heads - 1)
        def _():
            start(c_copies(unit, k, False))

    def advance(unit, k):
        forward(unit, k)

        @pl.when(unit + window < units)
        def _():
            start(z_copies(unit + window, k))

    def stage_b(unit):
        head, part = unit // CUTS, unit % CUTS

        @pl.when(part == 0)
        def _():
            for copy in y_own_arrival(head):
                copy.wait_recv()
            start(c_head(head, 0, True))

        for k in (3, 1, 2):
            for copy in y_copies(unit, k):
                copy.wait_recv()

        @pl.when(head == heads - 1)
        def _():
            for k in (3, 1, 2):
                start(c_copies(unit, k, True))

        @pl.when((head < heads - 1) & (part == CUTS - 1))
        def _():
            for k in (3, 1, 2):
                start(c_head(head, k, False))
                start(c_head(head, k, True))

    def load_copies(head):
        pos = head % 2
        copies = [
            pltpu.make_async_copy(
                wq_all.at[head, i],
                slot_qkv.at[:, pl.ds(pl.multiple_of((pos * 3 + i) * HD, HD), HD)],
                load_sem.at[pos, i],
            )
            for i in range(3)
        ]
        copies.append(
            pltpu.make_async_copy(
                wo_all.at[head],
                slot_out.at[pl.ds(pl.multiple_of(pos * HD, HD), HD), :],
                load_sem.at[pos, 3],
            )
        )
        return copies

    def load(head):
        for copy in c_whole(head):
            copy.wait_recv()
        start(load_copies(head))

    def loaded(head):
        for copy in load_copies(head):
            copy.wait()

    q_gain = q_gain_ref[...]
    k_gain = k_gain_ref[...]
    blocks = SEQ // BLK

    def normalize_rows(first, count):
        step = 16

        def one(i, _):
            part = pl.ds(pl.multiple_of(first + i * step, step), step)
            values = normed[part, :].astype(jnp.float32)
            mean = jnp.mean(values, axis=-1, keepdims=True)
            centred = values - mean
            inverse = lax.rsqrt(jnp.mean(centred * centred, axis=-1, keepdims=True) + EPS)
            mean_ref[part, :] = mean
            inverse_ref[part, :] = inverse
            normed[part, :] = (centred * inverse * gain_ref[...]).astype(jnp.bfloat16)
            return 0

        lax.fori_loop(0, count // step, one, 0)

    def span_of(third, i):
        step = width // 6
        return pl.ds(pl.multiple_of((third * 2 + i) * step, step), step)

    def project(heads_of, third):
        cols = slice(heads_of[0] * 3 * HD, (heads_of[-1] + 1) * 3 * HD)

        @pl.when(third == 0)
        def _():
            qkv_sum[:, cols] = jnp.zeros_like(qkv_sum[:, cols])

        def one(i, _):
            part = span_of(third, i)
            qkv_sum[:, cols] += jnp.dot(
                normed[:, part], slot_qkv[part, cols], preferred_element_type=jnp.float32
            )
            return 0

        lax.fori_loop(0, 2, one, 0)

    def project_up(heads_of, third):
        cols = slice(heads_of[0] * HD, (heads_of[-1] + 1) * HD)

        @pl.when(third == 0)
        def _():
            up_sum[:, cols] = jnp.zeros_like(up_sum[:, cols])

        def one(i, _):
            part = span_of(third, i)
            up_sum[:, cols] += lax.dot_general(
                grads[:, part], slot_out[cols, part], (((1,), (1,)), ((), ())),
                preferred_element_type=jnp.float32,
            )
            return 0

        lax.fori_loop(0, 2, one, 0)

    def attend(pair, which):
        def one(image, _):
            part = pl.ds(pl.multiple_of(image * SEQ, SEQ), SEQ)
            cols = [pl.ds(pl.multiple_of((which * 3 + j) * HD, HD), HD) for j in range(3)]
            up_cols = pl.ds(pl.multiple_of(which * HD, HD), HD)
            results = head_grads(
                qkv_sum[part, cols[0]].astype(jnp.bfloat16).astype(jnp.float32),
                qkv_sum[part, cols[1]].astype(jnp.bfloat16).astype(jnp.float32),
                qkv_sum[part, cols[2]].astype(jnp.bfloat16),
                up_sum[part, up_cols].astype(jnp.bfloat16),
                q_gain, k_gain,
                lambda i, s: pattern_ref[((p * heads + 2 * pair + which) * blocks + i) * ksel + s],
                ksel,
            )
            for j in range(3):
                d_qkv[part, cols[j]] = results[j]
            return 0

        lax.fori_loop(0, 2 * rows // SEQ, one, 0)

    def add_cols(which, part_of, of_rows=slice(None)):
        step = 512
        base = which * half + part_of * quarter

        def one(i, _):
            part = pl.ds(pl.multiple_of(base + i * step, step), step)
            total[of_rows, part] += lax.dot_general(
                d_qkv[of_rows, :], slot_qkv[part, :], (((1,), (1,)), ((), ())),
                preferred_element_type=jnp.float32,
            )
            return 0

        lax.fori_loop(0, quarter // step, one, 0)

    act_z(0).start()
    act_x(0).start()

    def each_head(act, low=0, high=heads):
        def one(head, _):
            act(head)
            return 0

        lax.fori_loop(low, high, one, 0)

    @pl.when(inner)
    def _():
        each_head(lambda unit: start(z_copies(unit, 3)), 0, units)

    each_head(forward_own)
    each_head(lambda head: start(own_copies(head, False)))
    for i in range(2):
        act_local(i).start()
    tok_copy = pltpu.make_async_copy(tok_hbm, tok_own, local_sem.at[2])
    tok_copy.start()
    total[...] = jnp.zeros_like(total)

    def turn_own(head):
        for copy in own_copies(head, False):
            copy.wait()
        start(own_copies(head, True))

    each_head(turn_own)

    @pl.when(inner)
    def _():
        each_head(lambda unit: forward(unit, 3), 0, units // 2)

    act_z(0).wait_send()
    act_z(1).start()
    act_z(0).wait_recv()
    act_forward(0).start()
    act_x(1).start()

    @pl.when(inner)
    def _():
        each_head(lambda unit: forward(unit, 3), units // 2, units)

    act_z(1).wait_recv()
    act_forward(1).start()
    act_z(1).wait_send()

    def first_units(unit):
        for k in (1, 2):
            start(z_copies(unit, k))

        @pl.when(jnp.logical_not(inner))
        def _():
            start(z_copies(unit, 3))

    each_head(first_units, 0, window)

    def wait_own(head):
        for copy in own_copies(head, True):
            copy.wait()

    each_head(wait_own)

    def third_step(t):
        unit, k = t // 3, t % 3

        @pl.when(k == 0)
        def _():
            advance(unit, 1)

        @pl.when(k == 1)
        def _():
            advance(unit, 2)

        @pl.when((k == 2) & jnp.logical_not(inner))
        def _():
            advance(unit, 3)

        @pl.when((k == 2) & (unit > 0) & (unit % CUTS == 0))
        def _():
            each_head(stage_b, unit - CUTS, unit)

        @pl.when((k == 2) & (unit > units - CUTS))
        def _():
            stage_b(unit - 1)

        def arrived(i):
            act_local(i).wait()
            act_x(i).wait()
            act_forward(i).wait()

        @pl.when(t == 2)
        def _():
            arrived(0)

        @pl.when((t >= 3) & (t < 7))
        def _():
            normalize_rows((t - 3) * (rows // 2), rows // 2)

        @pl.when(t == 18)
        def _():
            load(0)

        @pl.when(t == 29)
        def _():
            load(1)

        @pl.when(t == 31)
        def _():
            loaded(0)
            loaded(1)

        @pl.when(t == 55)
        def _():
            loaded(2)
            loaded(3)

        @pl.when(((t >= 31) & (t < 34)) | ((t >= 55) & (t < 58)))
        def _():
            project((0, 1), (t - 31) % 24)

        @pl.when(t == 40)
        def _():
            arrived(1)

        @pl.when((t == 40) | (t == 58))
        def _():
            each_head(lambda third: project_up((0, 1), third), 0, 3)

        @pl.when((t == 41) | (t == 42) | (t == 59) | (t == 60) | (t == 71))
        def _():
            attend((t - 39) // 16, (t + 1) % 2)

        @pl.when((t == 43) | (t == 44) | (t == 61) | (t == 62))
        def _():
            add_cols((t + 1) % 2, 0)
            add_cols((t + 1) % 2, 1)

        @pl.when(t == 45)
        def _():
            load(2)

        @pl.when(t == 53)
        def _():
            load(3)

        @pl.when(t == 65)
        def _():
            load(4)

        @pl.when(t == 67)
        def _():
            loaded(4)

        @pl.when((t >= 67) & (t < 70))
        def _():
            project((0,), t - 67)
            project_up((0,), t - 67)

    each_head(third_step, 0, 3 * units)
    tok_copy.wait()
    stage_b(units - 1)
    load(5)
    loaded(5)
    for third in range(3):
        project((1,), third)
        project_up((1,), third)
    attend(2, 1)

    def block_cols(which, part):
        return pl.ds(pl.multiple_of(which * half + part * quarter, quarter), quarter)

    def reduce_leg(i, src, dst, peer):
        return remote(src, dst, r_send.at[i], r_recv.at[i], peer)

    x_legs = [reduce_leg(i, x_out.at[r], x_in.at[r], x_peer) for i, r in enumerate((pair_rows, own_rows))]
    z_legs = [
        reduce_leg(2 + i, z_out.at[w], z_in.at[w], z_peer[1]) for i, w in enumerate((1 - x, x))
    ]
    z_last = reduce_leg(4, z_out2, z_in2, z_peer[1])
    x_last = reduce_leg(5, x_out2, x_in2, x_peer)
    add_cols(1 - x, 0, pair_rows)
    x_out[pair_rows, :] = total[pair_rows, block_cols(1 - x, 0)].astype(jnp.bfloat16)
    x_legs[0].start()
    add_cols(1 - x, 1, pair_rows)
    z_out[1 - x] = total[pair_rows, block_cols(1 - x, 1)].astype(jnp.bfloat16)
    z_legs[0].start()
    add_cols(1 - x, 0, own_rows)
    x_out[own_rows, :] = total[own_rows, block_cols(1 - x, 0)].astype(jnp.bfloat16)
    x_legs[1].start()
    add_cols(x, 1, pair_rows)
    z_out[x] = total[pair_rows, block_cols(x, 1)].astype(jnp.bfloat16)
    z_legs[1].start()
    add_cols(1 - x, 1, own_rows)
    add_cols(x, 1, own_rows)
    add_cols(x, 0, pair_rows)
    add_cols(x, 0, own_rows)

    step = 16
    lane = lax.broadcasted_iota(jnp.int32, (step, 128), 1)

    def sum_rows(i):
        part = pl.ds(pl.multiple_of(i * step, step), step)
        share = total[part, :]
        first = jnp.sum(share * gain_ref[...], axis=-1, keepdims=True)
        second = jnp.sum(share * normed[part, :].astype(jnp.float32), axis=-1, keepdims=True)
        sums[part, :] = jnp.where(lane == 0, first, jnp.where(lane == 1, second, 0.0))

    each_head(sum_rows, 0, 2 * rows // step)
    sums_out[0] = sums[own_rows, :].T[:8]
    sums_out[1] = sums[pair_rows, :].T[:8]
    sum_legs = [
        reduce_leg(6, sums_out.at[0], sums_in.at[0], x_peer),
        reduce_leg(7, sums_out.at[1], sums_in.at[1], z_peer[1]),
        reduce_leg(8, sums_out.at[1], sums_in.at[2], far_peer),
    ]
    start(sum_legs)

    x_legs[0].wait_recv()
    z_out2[...] = (
        total[pair_rows, block_cols(x, 0)] + x_in[pair_rows, :].astype(jnp.float32)
    ).astype(jnp.bfloat16)
    z_last.start()
    z_legs[0].wait_recv()
    x_out2[...] = (
        total[own_rows, block_cols(1 - x, 1)] + z_in[1 - x].astype(jnp.float32)
    ).astype(jnp.bfloat16)
    x_last.start()
    for leg in sum_legs:
        leg.wait_recv()
    means = (sums_out[0] + sums_in[0] + sums_in[1] + sums_in[2]) / width
    sums[:rows, :] = jnp.concatenate([means, jnp.zeros((120, rows), jnp.float32)], axis=0).T
    x_legs[1].wait_recv()
    total[own_rows, block_cols(x, 0)] += x_in[own_rows, :].astype(jnp.float32)
    z_legs[1].wait_recv()
    total[own_rows, block_cols(x, 1)] += z_in[x].astype(jnp.float32)

    def finish(part_of, arrived):
        cols = block_cols(x, part_of)
        here = slice(part_of * quarter, (part_of + 1) * quarter)

        def one(i):
            part = pl.ds(pl.multiple_of(i * step, step), step)
            shifted = pl.ds(pl.multiple_of(p * rows + i * step, step), step)
            inverse = inverse_ref[shifted, :]
            hat = (tok_own[part, here].astype(jnp.float32) - mean_ref[shifted, :]) * inverse
            d_hat = (total[shifted, cols] + arrived[part, :].astype(jnp.float32)) * gain_ref[:, cols]
            row_means = sums[part, :]
            out_ref[part, here] = (
                inverse * (d_hat - row_means[:, :1] - hat * row_means[:, 1:2])
            ).astype(jnp.bfloat16)

        each_head(one, 0, rows // step)

    z_last.wait_recv()
    finish(0, z_in2)
    x_last.wait_recv()
    finish(1, x_in2)

    for copy in (*x_legs, *z_legs, z_last, x_last, *sum_legs):
        copy.wait_send()

    def drain(unit):
        for k in (1, 2, 3):
            for copy in (*z_copies(unit, k), *y_copies(unit, k)):
                copy.wait_send()

    each_head(drain, 0, units)

    def drain_core(head):
        for copy in y_own(head):
            copy.wait_send()
        for copy in c_whole(head):
            copy.wait_send()

    each_head(drain_core)


def fused_body(tokens, grad_out, input_norm_gain, q_gain, k_gain, w_qkv, w_out, pattern):
    rows, half = tokens.shape
    depth = w_qkv.shape[1]
    width = 2 * half
    heads = w_qkv.shape[2] // HD // 2
    quarter = half // 2
    dma = pltpu.SemaphoreType.DMA
    bf16, f32 = jnp.bfloat16, jnp.float32
    vmem = pl.BlockSpec(memory_space=pltpu.VMEM)
    hbm = pl.BlockSpec(memory_space=pl.ANY)
    return pl.pallas_call(
        functools.partial(fused_kernel, heads, pattern.shape[2]),
        out_shape=[
            jax.ShapeDtypeStruct((rows, half), bf16),
            jax.ShapeDtypeStruct((heads, 3, width, HD), bf16),
            jax.ShapeDtypeStruct((heads, HD, width), bf16),
        ],
        in_specs=[pl.BlockSpec(memory_space=pltpu.SMEM), vmem, vmem, vmem, hbm, hbm, hbm, hbm],
        out_specs=[vmem, hbm, hbm],
        scratch_shapes=[
            pltpu.VMEM((2 * rows, width), bf16),
            pltpu.VMEM((2 * rows, width), bf16),
            pltpu.VMEM((rows, half), bf16),
            pltpu.VMEM((2 * rows, width), f32),
            pltpu.VMEM((width, 6 * HD), bf16),
            pltpu.VMEM((2 * HD, width), bf16),
            pltpu.VMEM((2 * rows, 6 * HD), f32),
            pltpu.VMEM((2 * rows, 2 * HD), f32),
            pltpu.VMEM((2 * rows, 6 * HD), bf16),
            pltpu.VMEM((2 * rows, 1), f32),
            pltpu.VMEM((2 * rows, 1), f32),
            pltpu.VMEM((2 * rows, quarter), bf16),
            pltpu.VMEM((2 * rows, quarter), bf16),
            pltpu.VMEM((2, rows, quarter), bf16),
            pltpu.VMEM((2, rows, quarter), bf16),
            pltpu.VMEM((rows, quarter), bf16),
            pltpu.VMEM((rows, quarter), bf16),
            pltpu.VMEM((rows, quarter), bf16),
            pltpu.VMEM((rows, quarter), bf16),
            pltpu.VMEM((2 * rows, 128), f32),
            pltpu.VMEM((2, 8, rows), f32),
            pltpu.VMEM((3, 8, rows), f32),
            dma((3,)),
            dma((2, 3)),
            dma((2, 3)),
            dma((heads * CUTS, 3, 2)),
            dma((heads * CUTS, 3, 2)),
            dma((heads * CUTS, 4, 2)),
            dma((heads * CUTS, 4, 2)),
            dma((heads, 2)),
            dma((heads, 2)),
            dma((heads, 4)),
            dma((2, 4)),
            dma((9,)),
            dma((9,)),
        ],
        compiler_params=pltpu.CompilerParams(
            collective_id=0, has_side_effects=True, vmem_limit_bytes=60 * 1024 * 1024
        ),
        cost_estimate=pl.CostEstimate(
            flops=14 * 2 * rows * width * heads * HD,
            bytes_accessed=16 * width * heads * HD,
            transcendentals=2 * rows * heads * SEQ,
        ),
        name="fused",
    )(
        pattern.reshape(-1), input_norm_gain.reshape(1, width), q_gain.reshape(1, HD),
        k_gain.reshape(1, HD), tokens, grad_out, w_qkv, w_out,
    )[0]


def choose(*args):
    fits = lax.axis_size("dp") == 16 and lax.axis_size("tensor") == 2
    fits = fits and args[0].shape[0] == SEQ and args[5].shape[2] == 12 * HD
    return (fused_body if fits else body)(*args)


def solution(mesh):
    return jax.shard_map(
        choose,
        mesh=mesh,
        in_specs=(
            P("dp", "tensor"),
            P("dp", "tensor"),
            P(),
            P(),
            P(),
            P(None, "dp", "tensor"),
            P("tensor", "dp"),
            P("tensor", None, None),
        ),
        out_specs=P("dp", "tensor"),
        check_vma=False,
    )
```
